512 devices in a mesh: fz: 32 (over y, x, core), fxy: 16 (over z).
Axes of the slice: x: 4, y: 4, z: 16, core: 2. Of those that a mesh axis runs over, the one named last changes fastest.
Arguments:
- e_field: float32 [3, 256, 256, 512], P(None, 'fz', 'fxy'), may hold values from -6 to 6
- h_field: float32 [3, 256, 256, 512], P(None, 'fz', 'fxy'), may hold values from -6 to 6
- e_decay: float32 [256, 256, 512], P('fz', 'fxy'), may hold values from 0.6 to 1
- e_gain: float32 [256, 256, 512], P('fz', 'fxy'), may hold values from 0.2 to 0.6
- port_cell: int32 [32, 1024], P('fz', 'fxy'), may hold values from 0 to 65535
- port_node: int32 [32, 1024], P('fz', 'fxy'), may hold values from 0 to 2047
- port_conductance: float32 [32, 1024], P('fz', 'fxy'), may hold values from 0.5 to 2
- inverse: float32 [32, 2048, 2048], P('fz', 'fxy'), may hold values from -1 to 2, as said below
- line_near: int32 [32, 128], P('fz'), may hold values from 0 to 2047
- line_far: int32 [32, 128], P('fz'), may hold values from 0 to 2047
- line_delay: int32 [32, 128], P('fz'), may hold values from 1 to 6
- line_imped: float32 [32, 128], P('fz'), may hold values from 0.5 to 4
- hist_near: float32 [32, 6, 128], P('fz'), may hold values from -6 to 6
- hist_far: float32 [32, 6, 128], P('fz'), may hold values from -6 to 6
Outputs:
- e_out: float32 [3, 256, 256, 512], P(None, 'fz', 'fxy')
- h_out: float32 [3, 256, 256, 512], P(None, 'fz', 'fxy')
- node_volt: float32 [32, 2048], P('fz', 'fxy')
- line_wave: float32 [32, 2, 128], P('fz')
The draws below stay inside these ranges and needn't reach their ends.
Inputs may be any that keep to these rules, and one draw needn't show every extreme that they name: inverse[s] is symmetric for every s.
All inputs are finite; a program needn't handle non-finite values.
Results may differ from the reference program's by a relative error of at most 0.00029.
Values sent between devices are 32-bit elements; how exact they have to be, the bound alone decides.
No kernel may reach another device: no remote copies, remote signals or barrier semaphores. Data moves between devices by JAX's collectives and lax.ppermute only.
A program may use at most 64 MiB of HBM per device.

```python
import math
import jax
import jax.numpy as jnp
from jax import lax

CZ = 8
CX = 16
NY = 512
NODES = 2048
PORTS_DEV = 64
LINES = 128
DMAX = 6
STEPS = 4
NZ = 256
NX = 256
PORTS = 1024
N_FZ = 32


def draw_inverse(key, part):
    first, second = jax.random.split(jax.random.fold_in(key, 7))
    noise = jax.random.normal(first, (N_FZ, NODES, NODES), jnp.float32)
    symmetric = (noise + jnp.swapaxes(noise, 1, 2)) * (0.3 / math.sqrt(2.0 * NODES))
    diagonal = jax.random.uniform(second, (N_FZ, NODES), jnp.float32, 0.8, 1.2)
    return symmetric + diagonal[:, :, None] * jnp.eye(NODES, dtype=jnp.float32)


def with_ends(drawn, own_key, low, high):
    extent = drawn.shape
    place = [jax.random.randint(jax.random.fold_in(own_key, axis), (), 0, extent[axis]) for axis in range(len(extent))]
    drawn = drawn.at[tuple(place)].set(low)
    longest = extent.index(max(extent))
    place[longest] = (place[longest] + 1) % extent[longest]
    return drawn.at[tuple(place)].set(high)


def steps_of(key, shape, pieces, least, high):
    gain, own = 1.0, jax.random.fold_in(key, 6)
    for dim, parts in pieces:
        heights = jnp.exp(jax.random.uniform(jax.random.fold_in(own, dim), (parts,), jnp.float32, least / len(pieces), high / len(pieces)))
        gain = gain * jnp.repeat(heights, shape[dim] // parts).reshape([-1 if axis == dim else 1 for axis in range(len(shape))])
    return gain


def scatter_about(rng, dims, deviation, limit, cuts=(), held_as=jnp.bfloat16):
    array = jax.random.normal(rng, dims, jnp.float32) * deviation
    if len(cuts) > 0:
        array = steps_of(rng, dims, cuts, -0.22, 0.18) * array
    return jnp.clip(array, min=-limit, max=limit).astype(held_as)


def setup_inputs(seed: int = 0) -> dict:
    splits = jax.random.split(jax.random.key(seed), 15)
    e_field = scatter_about(splits[0], (3, NZ, NX, NY), 1.0, 6.0, ((1, 32), (2, 16)), jnp.float32)
    h_field = scatter_about(splits[1], (3, NZ, NX, NY), 1.0, 6.0, ((1, 32), (2, 16)), jnp.float32)
    e_decay = jnp.clip(0.6 + 0.39999998 * jax.random.uniform(splits[2], (NZ, NX, NY), jnp.float32) ** steps_of(splits[2], (NZ, NX, NY), ((0, 32), (1, 16)), -0.2, 0.2), 0.6, 1.0)
    e_gain = jnp.clip(0.2 + 0.400000021 * jax.random.uniform(splits[3], (NZ, NX, NY), jnp.float32) ** steps_of(splits[3], (NZ, NX, NY), ((0, 32), (1, 16)), -0.2, 0.2), 0.2, 0.6)
    port_cell = with_ends(jax.random.randint(splits[4], (N_FZ, PORTS), 0, CZ * CX * NY), jax.random.fold_in(splits[4], 1), 0, (CZ * CX * NY) - 1).astype(jnp.int32)
    port_node = with_ends(jax.random.randint(splits[5], (N_FZ, PORTS), 0, NODES), jax.random.fold_in(splits[5], 1), 0, NODES - 1).astype(jnp.int32)
    port_conductance = jnp.clip(jnp.exp(math.log(2.0) - 1.3862944 * jax.random.uniform(splits[6], (N_FZ, PORTS), jnp.float32) ** steps_of(splits[6], (N_FZ, PORTS), ((0, 32), (1, 16)), -0.2, 0.2)), 0.5, 2.0)
    inverse = draw_inverse(jax.random.fold_in(splits[14], 71), 0)
    line_near = with_ends(jax.random.randint(splits[8], (N_FZ, LINES), 0, NODES), jax.random.fold_in(splits[8], 1), 0, NODES - 1).astype(jnp.int32)
    line_far = with_ends(jax.random.randint(splits[9], (N_FZ, LINES), 0, NODES), jax.random.fold_in(splits[9], 1), 0, NODES - 1).astype(jnp.int32)
    line_delay = with_ends(jax.random.randint(splits[10], (N_FZ, LINES), 1, DMAX + 1), jax.random.fold_in(splits[10], 1), 1, DMAX).astype(jnp.int32)
    line_imped = jnp.clip(jnp.exp(math.log(4.0) - 2.0794415 * jax.random.uniform(splits[11], (N_FZ, LINES), jnp.float32) ** steps_of(splits[11], (N_FZ, LINES), ((0, 32),), -0.2, 0.2)), 0.5, 4.0)
    hist_near = scatter_about(splits[12], (N_FZ, DMAX, LINES), 1.0, 6.0, ((0, 32),), jnp.float32)
    hist_far = scatter_about(splits[13], (N_FZ, DMAX, LINES), 1.0, 6.0, ((0, 32),), jnp.float32)
    return {"e_field": e_field, "h_field": h_field, "e_decay": e_decay, "e_gain": e_gain, "port_cell": port_cell, "port_node": port_node, "port_conductance": port_conductance, "inverse": inverse, "line_near": line_near, "line_far": line_far, "line_delay": line_delay, "line_imped": line_imped, "hist_near": hist_near, "hist_far": hist_far}


def forward_z(values, upper_face):
    return jnp.concatenate([values[1:], upper_face[None]], 0) - values


def forward_x(values, side_face):
    return jnp.concatenate([values[:, 1:], side_face[:, None]], 1) - values


def forward_y(values):
    return jnp.concatenate([values[:, :, 1:], jnp.zeros_like(values[:, :, :1])], 2) - values


def backward_z(values, lower_face):
    return values - jnp.concatenate([lower_face[None], values[:-1]], 0)


def backward_x(values, side_face):
    return values - jnp.concatenate([side_face[:, None], values[:, :-1]], 1)


def backward_y(values):
    return values - jnp.concatenate([jnp.zeros_like(values[:, :, :1]), values[:, :, :-1]], 2)


def curl_electric(e_field, upper_face, side_face):
    return jnp.stack([
        forward_y(e_field[2]) - forward_z(e_field[1], upper_face[1]),
        forward_z(e_field[0], upper_face[0]) - forward_x(e_field[2], side_face[1]),
        forward_x(e_field[1], side_face[0]) - forward_y(e_field[0])])


def curl_magnetic(h_field, lower_face, side_face):
    return jnp.stack([
        backward_y(h_field[2]) - backward_z(h_field[1], lower_face[1]),
        backward_z(h_field[0], lower_face[0]) - backward_x(h_field[2], side_face[1]),
        backward_x(h_field[1], side_face[0]) - backward_y(h_field[0])])


def reference(e_field, h_field, e_decay, e_gain, port_cell, port_node, port_conductance, inverse,
              line_near, line_far, line_delay, line_imped, hist_near, hist_far):
    row_index = jnp.arange(N_FZ, dtype=jnp.int32)[:, None]
    block_index = jnp.arange(PORTS, dtype=jnp.int32)[None, :] // PORTS_DEV
    z_position = row_index * CZ + port_cell // (CX * NY)
    x_position = block_index * CX + (port_cell // NY) % CX
    y_position = port_cell % NY
    flat_index = ((z_position * NX + x_position) * NY + y_position).astype(jnp.int32)
    gain_flat = e_gain.reshape(-1)
    wave_near = hist_near[:, ::-1]
    wave_far = hist_far[:, ::-1]
    upper_zero = jnp.zeros((2, NX, NY), jnp.float32)
    side_zero = jnp.zeros((2, NZ, NY), jnp.float32)
    empty_nodes = jnp.zeros((N_FZ, NODES), jnp.float32)
    for step_index in range(STEPS):
        position = (step_index - line_delay + DMAX).astype(jnp.int32)[:, None, :]
        incoming_a = jnp.take_along_axis(wave_far, position, axis=1)[:, 0]
        incoming_b = jnp.take_along_axis(wave_near, position, axis=1)[:, 0]
        far_sources = empty_nodes.at[row_index, line_far].add(-incoming_b)
        received = jnp.concatenate([jnp.zeros((1, NODES), jnp.float32), far_sources[:-1]], 0)
        ez_ports = e_field[2].reshape(-1)[flat_index]
        sources = empty_nodes.at[row_index, port_node].add(port_conductance * ez_ports)
        sources = sources + empty_nodes.at[row_index, line_near].add(-incoming_a) + received
        volts = jnp.einsum("snm,sm->sn", inverse, sources, precision=lax.Precision.HIGHEST)
        current = port_conductance * (ez_ports - volts[row_index, port_node])
        e_field = e_decay * e_field + e_gain * curl_magnetic(h_field, upper_zero, side_zero)
        vertical = e_field[2].reshape(-1).at[flat_index].add(-gain_flat[flat_index] * current)
        e_field = e_field.at[2].set(vertical.reshape(e_field.shape[1:]))
        out_near = -2.0 * volts[row_index, line_near] / line_imped - incoming_a
        volts_above = jnp.concatenate([volts[1:], jnp.zeros((1, NODES), jnp.float32)], 0)
        out_far = -2.0 * volts_above[row_index, line_far] / line_imped - incoming_b
        h_field = h_field - 0.5 * curl_electric(e_field, upper_zero, side_zero)
        wave_near = jnp.concatenate([wave_near, out_near[:, None]], 1)
        wave_far = jnp.concatenate([wave_far, out_far[:, None]], 1)
    line_wave = jnp.stack([out_near, out_far], 1)
    return e_field, h_field, volts, line_wave
```

```python
import functools

import jax
import jax.numpy as jnp
from jax import lax
from jax.experimental import pallas as pl
from jax.experimental.pallas import tpu as pltpu
from jax.sharding import PartitionSpec as P

STEPS = 4
F32 = jnp.float32
BF16 = jnp.bfloat16
NZ = 8
NX = 16
NY = 512
GX = 24
NF = 32
NB = 16
HALF = 64
LANES = 128
DEPTH = 6
VMEM = pl.BlockSpec(memory_space=pltpu.VMEM)
NT = (((1,), (1,)), ((), ()))


def call(kernel, outs, *args, alias=None, name=None):
    return pl.pallas_call(
        kernel,
        out_shape=[jax.ShapeDtypeStruct(s, d) for s, d in outs],
        in_specs=[VMEM] * len(args),
        out_specs=[VMEM] * len(outs),
        input_output_aliases=alias or {},
        name=name,
        compiler_params=pltpu.CompilerParams(vmem_limit_bytes=40 << 20),
    )(*args)


def shifted(value, axis, by):
    devices = lax.axis_size(axis)
    pairs = [(i, i + by) for i in range(devices) if 0 <= i + by < devices]
    return lax.ppermute(value, axis, pairs)


def exchanged(value):
    return lax.all_to_all(value, "fxy", 0, 0, tiled=True)


def iota(shape, dim):
    return lax.broadcasted_iota(jnp.int32, shape, dim)


def split3(value):
    high = value.astype(BF16)
    rest = value - high.astype(F32)
    middle = rest.astype(BF16)
    low = (rest - middle.astype(F32)).astype(BF16)
    return high, middle, low


def dot3(value, onehot, dims=(((1,), (0,)), ((), ()))):
    rows = value.shape[0]
    parts = jnp.concatenate(split3(value), 0)
    product = lax.dot_general(parts, onehot, dims, preferred_element_type=F32)
    return product[:rows] + (product[rows : 2 * rows] + product[2 * rows :])


def next_y(f):
    rolled = pltpu.roll(f, NY - 1, 1)
    return jnp.where(iota(f.shape, 1) == NY - 1, 0.0, rolled)


def last_y(f):
    rolled = pltpu.roll(f, 1, 1)
    return jnp.where(iota(f.shape, 1) == 0, 0.0, rolled)


def next_x(f):
    return jnp.concatenate([f[1:], f[:1]], 0)


def last_x(f):
    return jnp.concatenate([f[GX - 1 :], f[: GX - 1]], 0)


def column():
    return lax.axis_index("fxy")


def row():
    return lax.axis_index("fz")


def half_mask():
    lane = iota((1, LANES), 1)
    return (lane // HALF == column() // 8).astype(F32)


def own_onehots(cell):
    mine = half_mask() > 0.5
    rows = iota((NZ * NX, LANES), 0) == cell // NY
    at_row = jnp.where(rows & mine, 1.0, 0.0).astype(BF16)
    at_y = jnp.where(iota((NY, LANES), 0) == cell % NY, 1.0, 0.0).astype(BF16)
    return at_row, at_y


def at_ports(field, at_row, at_y):
    picked = dot3(field, at_y)
    return jnp.sum(picked * at_row.astype(F32), 0, keepdims=True)


def hist_at(hist, position):
    out = jnp.zeros((1, LANES), F32)
    for k in range(DEPTH + STEPS):
        out = jnp.where(position == k, hist[k : k + 1], out)
    return out


def k_first(e_ref, h_ref, g_ref, cell_ref, node_ref, cond_ref, far_ref, delay_ref, imped_ref, near_hist_ref, pay_ref, up_ref, right_ref):
    def packed(ref):
        value = ref[...].astype(F32)
        return jnp.concatenate([value, value], 1) * half_mask()

    cell = packed(cell_ref)
    at_row, at_y = own_onehots(cell.astype(jnp.int32))
    ez = at_ports(e_ref[2].reshape(NZ * NX, NY), at_row, at_y)
    gain = at_ports(g_ref[...].reshape(NZ * NX, NY), at_row, at_y)
    rows = [packed(node_ref), cell, packed(cond_ref), ez, gain, jnp.zeros((3, LANES), F32)]
    pay_ref[...] = jnp.broadcast_to(jnp.concatenate(rows, 0)[None], (NB, 8, LANES))
    up_ref[0:NX] = h_ref[0, NZ - 1]
    up_ref[NX : 2 * NX] = h_ref[1, NZ - 1]
    static = [far_ref[...].astype(F32), delay_ref[...].astype(F32), imped_ref[...], jnp.zeros((5, LANES), F32)]
    hist = [near_hist_ref[0], jnp.zeros((2, LANES), F32)]
    up_ref[2 * NX :, 0:LANES] = jnp.concatenate(static, 0)
    up_ref[2 * NX :, LANES : 2 * LANES] = jnp.concatenate(hist, 0)
    up_ref[2 * NX :, 2 * LANES :] = jnp.zeros((8, NY - 2 * LANES), F32)
    for c in range(2):
        for z in range(NZ):
            right_ref[c * NZ + z : c * NZ + z + 1] = h_ref[1 + c, z, NX - 1 : NX]


def curl_z(h_ref, z):
    hx, hy = h_ref[0, z + 1], h_ref[1, z + 1]
    return ((hy - last_x(hy)) - (hx - last_y(hx)))[:NX]


def update_exy(old_ref, e_ref, h_ref, d_ref, g_ref, base):
    for z in range(NZ):
        hz = h_ref[2, z + 1]
        own = hz[:NX]
        curl_x = (own - last_y(own)) - (h_ref[1, z + 1, :NX] - h_ref[1, z, :NX])
        curl_y = (h_ref[0, z + 1, :NX] - h_ref[0, z, :NX]) - (hz - last_x(hz))[:NX]
        d, g = d_ref[z], g_ref[z]
        e_ref[0, z + 1, :NX] = d * old_ref[0, z + base, :NX] + g * curl_x
        e_ref[1, z + 1, :NX] = d * old_ref[1, z + base, :NX] + g * curl_y


def update_ez(old_ref, e_ref, h_ref, d_ref, g_ref, base):
    for z in range(NZ):
        e_ref[2, z + 1, :NX] = d_ref[z] * old_ref[2, z + base, :NX] + g_ref[z] * curl_z(h_ref, z)


def send_x(e_ref, right_ref, left_ref):
    for z in range(NZ):
        for c in range(3):
            right_ref[c * NZ + z : c * NZ + z + 1] = e_ref[c, z + 1, NX - 1 : NX]
        for c in range(2):
            left_ref[c * NZ + z : c * NZ + z + 1] = e_ref[1 + c, z + 1, 0:1]


def k_start(e_in, h_in, d_ref, g_ref, cell_ref, up_ref, right_ref, e_ref, h_ref, pre_ref, xr_ref, xl_ref):
    first = iota((8, NY), 0)
    for z in range(NZ):
        for c in range(3):
            h_ref[c, z + 1, :NX] = h_in[c, z]
            if c:
                ghost = right_ref[(c - 1) * NZ + z : (c - 1) * NZ + z + 1]
                h_ref[c, z + 1, NX:] = jnp.where(first == 7, ghost, 0.0)
            else:
                h_ref[c, z + 1, NX:] = jnp.zeros((8, NY), F32)
    for c in range(3):
        h_ref[c, 0] = jnp.zeros((GX, NY), F32)
        e_ref[c, 0] = jnp.zeros((GX, NY), F32)
        e_ref[c, NZ + 1] = jnp.zeros((GX, NY), F32)
    h_ref[0, 0, :NX] = up_ref[0:NX]
    h_ref[1, 0, :NX] = up_ref[NX : 2 * NX]
    update_ez(e_in, e_ref, h_ref, d_ref, g_ref, 0)
    update_exy(e_in, e_ref, h_ref, d_ref, g_ref, 0)
    cell = cell_ref[...]
    at_row, at_y = own_onehots(jnp.concatenate([cell, cell], 1))
    pre = at_ports(e_ref[2, 1 : NZ + 1, :NX].reshape(NZ * NX, NY), at_row, at_y)
    pre_ref[...] = jnp.broadcast_to(pre, (8, LANES))
    send_x(e_ref, xr_ref, xl_ref)


def own_volts(w, lines, node, inverse_ref, onehot_ref):
    high = node // LANES
    sources = jnp.zeros((NB, LANES), F32)
    values = jnp.concatenate([w, lines], 0)
    for t in range(10):
        spread = jnp.where(iota((NB, LANES), 0) == high[t : t + 1], values[t : t + 1], 0.0)
        sources = sources + dot3(spread, onehot_ref[t], NT)
    total = jnp.zeros((LANES, LANES), F32)
    for t in range(NB):
        total = total + inverse_ref[0, :, t * LANES : (t + 1) * LANES] * sources[t : t + 1]
    return jnp.sum(total.T, 0, keepdims=True)


def node_values(volts, node, onehot_ref):
    high = node // LANES
    rows = []
    for t in range(10):
        picked = dot3(volts, onehot_ref[t])
        rows.append(jnp.sum(jnp.where(iota((NB, LANES), 0) == high[t : t + 1], picked, 0.0), 0, keepdims=True))
    return jnp.concatenate(rows, 0)


def line_inputs(static, hist, n):
    own = n - static[4:5].astype(jnp.int32) + DEPTH
    below = n - static[5:6].astype(jnp.int32) + DEPTH
    return hist_at(hist[16:32], own), hist_at(hist[32:48], below), hist_at(hist[0:16], own)


def payload(pay_ref, volts, pre):
    rows = jnp.concatenate([volts, pre, jnp.zeros((6, LANES), F32)], 0)
    pay_ref[...] = jnp.broadcast_to(rows[None], (NB, 8, LANES))


def k_tables(
    got_ref, up_ref, near_ref, delay_ref, imped_ref, near_hist_ref, far_hist_ref, inverse_ref, pre_ref, pay_ref, port_ref, onehot_ref, static_ref, hist_ref
):
    def packed(f):
        return got_ref[0:8, f, :] + got_ref[8:16, f, :]

    far_below = up_ref[2 * NX : 2 * NX + 1, 0:LANES]
    delay_below = up_ref[2 * NX + 1 : 2 * NX + 2, 0:LANES]
    imped_below = jnp.where(row() == 0, 1.0, up_ref[2 * NX + 2 : 2 * NX + 3, 0:LANES])
    near = near_ref[...].astype(F32)
    node = jnp.concatenate([packed(0), near, far_below, jnp.zeros((6, LANES), F32)], 0)
    port_ref[0:16] = node
    device = iota((8, LANES), 0) + 8 * (iota((8, LANES), 1) // HALF)
    port_ref[16:24] = packed(1) + (device * (NZ * NX * NY)).astype(F32)
    port_ref[24:32] = packed(2)
    port_ref[32:40] = packed(4)
    static = jnp.concatenate([near, far_below, imped_ref[...], imped_below, delay_ref[...].astype(F32), delay_below, jnp.zeros((2, LANES), F32)], 0)
    static_ref[...] = static
    hist_ref[...] = jnp.zeros((48, LANES), F32)
    for k in range(DEPTH):
        hist_ref[k : k + 1] = near_hist_ref[0, DEPTH - 1 - k : DEPTH - k]
        hist_ref[16 + k : 17 + k] = far_hist_ref[0, DEPTH - 1 - k : DEPTH - k]
        hist_ref[32 + k : 33 + k] = up_ref[2 * NX + DEPTH - 1 - k : 2 * NX + DEPTH - k, LANES : 2 * LANES]
    nodes = node.astype(jnp.int32)
    for t in range(10):
        onehot_ref[t] = jnp.where(iota((LANES, LANES), 0) == nodes[t : t + 1] % LANES, 1.0, 0.0).astype(BF16)
    into_near, into_below, _ = line_inputs(static, hist_ref[...], 0)
    ez = packed(3)
    port_ref[40:48] = ez
    w = packed(2) * ez
    volts = own_volts(w, -jnp.concatenate([into_near, into_below], 0), nodes, inverse_ref, onehot_ref)
    payload(pay_ref, volts, pre_ref[0:1])


def k_cells(port_ref, at_row_ref, at_y_ref):
    j = column()
    lane_high = iota((1, LANES), 1) // HALF
    for k in range(3):
        block = j + (k - 1)
        packed_row = jnp.where(block < 0, block + 8, block % 8)
        where = port_ref[pl.ds(16 + packed_row, 1), :].astype(jnp.int32)
        cell = where % (NZ * NX * NY)
        inside = (lane_high == block // 8) & (block >= 0) & (block < NB)
        x = (cell // NY) % NX + (k - 1) * NX
        position = jnp.where((x >= 0) & (x <= NX), x, jnp.where(x == -1, GX - 1, -1))
        target = jnp.where(inside & (position >= 0), (cell // (NX * NY)) * GX + position, -1)
        at_row_ref[:, k * LANES : (k + 1) * LANES] = jnp.where(iota((NZ * GX, LANES), 0) == target, 1.0, 0.0).astype(BF16)
        at_y_ref[:, k * LANES : (k + 1) * LANES] = jnp.where(iota((NY, LANES), 0) == cell % NY, 1.0, 0.0).astype(BF16)


def k_currents(
    n, last, got_ref, port_ref, ez_ref, onehot_ref, static_ref, hist_ref, at_row_ref, at_y_ref, xr_ref, xl_ref, e_in, e_ref, ez_out, wave_ref, *sends
):
    volts = got_ref[:, 0, :]
    pre = got_ref[0:8, 1, :] + got_ref[8:16, 1, :]
    node = port_ref[0:16].astype(jnp.int32)
    at_nodes = node_values(volts, node, onehot_ref)
    where = port_ref[16:24]
    cond = port_ref[24:32]
    current = cond * (ez_ref[...] - at_nodes[0:8])
    shared = current
    for k in range(1, LANES):
        same = pltpu.roll(where, k, 1) == where
        shared = shared + jnp.where(same, pltpu.roll(current, k, 1), 0.0)
    gain = port_ref[32:40]
    ez_out[...] = pre - gain * shared

    static = static_ref[...]
    into_near, into_below, into_own = line_inputs(static, hist_ref[...], n)
    out_near = -2.0 * at_nodes[8:9] / static[2:3] - into_near
    out_below = -2.0 * at_nodes[9:10] / static[3:4] - into_below
    top = jnp.where(row() == NF - 1, -into_own, 0.0)
    wave_ref[...] = jnp.concatenate([out_near, top, jnp.zeros((6, LANES), F32)], 0)

    first = iota((8, NY), 0)
    for z in range(NZ):
        for c in range(3):
            ghost = jnp.where(first == 7, xr_ref[c * NZ + z : c * NZ + z + 1], 0.0)
            if c:
                ghost = jnp.where(first == 0, xl_ref[(c - 1) * NZ + z : (c - 1) * NZ + z + 1], ghost)
            e_ref[c, z + 1, NX:] = ghost
    j = column()
    drop = gain * current
    block_rows = []
    for k in range(3):
        block = j + (k - 1)
        packed_row = jnp.where(block < 0, block + 8, block % 8)
        mask = iota((8, LANES), 0) == packed_row
        block_rows.append(jnp.sum(jnp.where(mask, drop, 0.0), 0, keepdims=True))
    drops = jnp.concatenate(block_rows, 1)
    at_row = at_row_ref[...]
    parts = jnp.concatenate([at_row * part for part in split3(drops)], 0)
    spread = lax.dot_general(parts, at_y_ref[...], NT, preferred_element_type=F32)
    rows = NZ * GX
    spread = spread[:rows] + (spread[rows : 2 * rows] + spread[2 * rows :])
    for z in range(NZ):
        e_ref[2, z + 1] = e_ref[2, z + 1] - spread[z * GX : (z + 1) * GX]

    down_ref = sends[-1]
    down_ref[0:GX] = e_ref[0, 1]
    down_ref[GX : GX + NX] = e_ref[1, 1, :NX]
    down_ref[GX + NX :] = jnp.zeros((8, NY), F32)
    down_ref[GX + NX : GX + NX + 1, 0:LANES] = out_below
    if not last:
        up_ref = sends[0]
        up_ref[0:NX] = e_ref[0, NZ, :NX]
        up_ref[NX : 2 * NX] = e_ref[1, NZ, :NX]
        up_ref[2 * NX : 2 * NX + GX] = e_ref[2, NZ]
        up_ref[2 * NX + GX :] = jnp.zeros((8, NY), F32)
        up_ref[2 * NX + GX : 2 * NX + GX + 1, 0:LANES] = out_near


def update_h(e_ref, h_ref, layer):
    scale = jnp.where((iota((GX, 1), 0) >= NX) & (column() == 0), 0.0, 0.5)
    ex, ey, ez = e_ref[0, layer], e_ref[1, layer], e_ref[2, layer]
    if layer == 0:
        scale = jnp.where(row() == 0, 0.0, scale)
    h_ref[0, layer] = h_ref[0, layer] - scale * ((next_y(ez) - ez) - (e_ref[1, layer + 1] - ey))
    h_ref[1, layer] = h_ref[1, layer] - scale * ((e_ref[0, layer + 1] - ex) - (next_x(ez) - ez))
    if layer:
        h_ref[2, layer] = h_ref[2, layer] - scale * ((next_x(ey) - ey) - (next_y(ex) - ex))


def k_inner_h(e_ref, h_in, h_ref):
    for layer in range(1, NZ):
        update_h(e_ref, h_ref, layer)


def edge_h(e_ref, h_ref, down_ref):
    e_ref[0, NZ + 1] = down_ref[0:GX]
    e_ref[1, NZ + 1, :NX] = down_ref[GX : GX + NX]
    update_h(e_ref, h_ref, NZ)


def k_volts(
    n, up_ref, down_ref, d_ref, g_ref, ez_ref, wave_ref, port_ref, onehot_ref, static_ref, inverse_ref, cell_ref, e_in, h_in, hist_in, e_ref, h_ref, hist_ref, pay_ref
):
    e_ref[0, 0, :NX] = up_ref[0:NX]
    e_ref[1, 0, :NX] = up_ref[NX : 2 * NX]
    e_ref[2, 0] = up_ref[2 * NX : 2 * NX + GX]
    update_h(e_ref, h_ref, 0)
    edge_h(e_ref, h_ref, down_ref)
    at = n - 1 + DEPTH
    hist_ref[at : at + 1] = wave_ref[0:1]
    hist_ref[16 + at : 17 + at] = down_ref[GX + NX : GX + NX + 1, 0:LANES] + wave_ref[1:2]
    hist_ref[32 + at : 33 + at] = up_ref[2 * NX + GX : 2 * NX + GX + 1, 0:LANES]
    into_near, into_below, _ = line_inputs(static_ref[...], hist_ref[...], n)
    lines = -jnp.concatenate([into_near, into_below], 0)
    w = port_ref[24:32] * ez_ref[...]
    volts = own_volts(w, lines, port_ref[0:16].astype(jnp.int32), inverse_ref, onehot_ref)
    update_ez(e_ref, e_ref, h_ref, d_ref, g_ref, 1)
    cell = cell_ref[...]
    at_row, at_y = own_onehots(jnp.concatenate([cell, cell], 1))
    pre = at_ports(e_ref[2, 1 : NZ + 1, :NX].reshape(NZ * NX, NY), at_row, at_y)
    payload(pay_ref, volts, pre)


def k_exy(h_ref, d_ref, g_ref, e_in, e_ref, xr_ref, xl_ref):
    update_exy(e_ref, e_ref, h_ref, d_ref, g_ref, 1)
    send_x(e_ref, xr_ref, xl_ref)


def k_last(down_ref, wave_ref, e_in, h_in, e_out, h_out, wave_out, e_ref, h_ref):
    edge_h(e_in, h_in, down_ref)
    for c in range(3):
        for z in range(NZ):
            e_out[c, z] = e_in[c, z + 1, :NX]
            h_out[c, z] = h_in[c, z + 1, :NX]
    above = down_ref[GX + NX : GX + NX + 1, 0:LANES] + wave_ref[1:2]
    wave_out[...] = jnp.concatenate([wave_ref[0:1], above], 0)[None]


def local(
    e_field,
    h_field,
    e_decay,
    e_gain,
    port_cell,
    port_node,
    port_conductance,
    inverse,
    line_near,
    line_far,
    line_delay,
    line_imped,
    hist_near,
    hist_far,
):
    e_shape = (3, NZ + 2, GX, NY)
    h_shape = (3, NZ + 1, GX, NY)
    pay_shape = (NB, 8, LANES)
    xr_shape, xl_shape = (3 * NZ, NY), (2 * NZ, NY)
    up_shape, down_shape = (2 * NX + GX + 8, NY), (NX + GX + 8, NY)

    pay, up, right = call(
        k_first,
        [(pay_shape, F32), ((2 * NX + 8, NY), F32), ((2 * NZ, NY), F32)],
        e_field, h_field, e_gain, port_cell, port_node, port_conductance, line_far, line_delay, line_imped, hist_near,
        name="first",
    )
    got = exchanged(pay)
    up = shifted(up, "fz", 1)
    right = shifted(right, "fxy", 1)
    e, h, pre, xr, xl = call(
        k_start,
        [(e_shape, F32), (h_shape, F32), ((8, LANES), F32), (xr_shape, F32), (xl_shape, F32)],
        e_field, h_field, e_decay, e_gain, port_cell, up, right,
        name="start",
    )
    pay, port, onehot, static, hist = call(
        k_tables,
        [(pay_shape, F32), ((48, LANES), F32), ((10, LANES, LANES), BF16), ((8, LANES), F32), ((48, LANES), F32)],
        got, up, line_near, line_delay, line_imped, hist_near, hist_far, inverse, pre,
        name="tables",
    )
    ez = port[40:48]
    at_row, at_y = call(k_cells, [((NZ * GX, 3 * LANES), BF16), ((NY, 3 * LANES), BF16)], port, name="cells")
    for n in range(STEPS):
        last = n == STEPS - 1
        if last:
            node_volt = pay[0, 0:1]
        got = exchanged(pay)
        xr = shifted(xr, "fxy", 1)
        xl = shifted(xl, "fxy", -1)
        sends = ([] if last else [(up_shape, F32)]) + [(down_shape, F32)]
        e, ez, wave, *sends = call(
            functools.partial(k_currents, n, last),
            [(e_shape, F32), ((8, LANES), F32), ((8, LANES), F32), *sends],
            got, port, ez, onehot, static, hist, at_row, at_y, xr, xl, e,
            alias={10: 0},
            name="currents",
        )
        down = shifted(sends[-1], "fz", -1)
        if not last:
            up = shifted(sends[0], "fz", 1)
        (h,) = call(k_inner_h, [(h_shape, F32)], e, h, alias={1: 0}, name="inner_h")
        if last:
            break
        e, h, hist, pay = call(
            functools.partial(k_volts, n + 1),
            [(e_shape, F32), (h_shape, F32), ((48, LANES), F32), (pay_shape, F32)],
            up, down, e_decay, e_gain, ez, wave, port, onehot, static, inverse, port_cell, e, h, hist,
            alias={11: 0, 12: 1, 13: 2},
            name="volts",
        )
        e, xr, xl = call(k_exy, [(e_shape, F32), (xr_shape, F32), (xl_shape, F32)], h, e_decay, e_gain, e, alias={3: 0}, name="exy")
    field = (3, NZ, NX, NY)
    e_out, h_out, line_wave, _, _ = call(
        k_last,
        [(field, F32), (field, F32), ((1, 2, LANES), F32), (e_shape, F32), (h_shape, F32)],
        down, wave, e, h,
        alias={2: 3, 3: 4},
        name="last",
    )
    return e_out, h_out, node_volt, line_wave


def solution(mesh):
    placed = (
        P(None, "fz", "fxy", None),
        P(None, "fz", "fxy", None),
        P("fz", "fxy", None),
        P("fz", "fxy", None),
        P("fz", "fxy"),
        P("fz", "fxy"),
        P("fz", "fxy"),
        P("fz", "fxy", None),
        P("fz", None),
        P("fz", None),
        P("fz", None),
        P("fz", None),
        P("fz", None, None),
        P("fz", None, None),
    )
    return jax.shard_map(
        local,
        mesh=mesh,
        in_specs=placed,
        out_specs=(
            P(None, "fz", "fxy", None),
            P(None, "fz", "fxy", None),
            P("fz", "fxy"),
            P("fz", None, None),
        ),
        check_vma=False,
    )
```

```python
import functools

import jax
import jax.numpy as jnp
from jax import lax
from jax.experimental import pallas as pl
from jax.experimental.pallas import tpu as pltpu
from jax.sharding import PartitionSpec as P

STEPS = 4
F32 = jnp.float32
BF16 = jnp.bfloat16
NZ = 8
NX = 16
NY = 512
GX = 24
NF = 32
NB = 16
HALF = 64
LANES = 128
DEPTH = 6
VMEM = pl.BlockSpec(memory_space=pltpu.VMEM)
ANY = pl.BlockSpec(memory_space=pl.ANY)
NT = (((1,), (1,)), ((), ()))
NODE, WHERE, COND, GAIN, EZ, STATIC, OWN, FROM_ABOVE, FROM_BELOW, WAVE, ROWS = 0, 16, 24, 32, 40, 48, 56, 72, 88, 104, 112
E_SHAPE = (3, NZ + 2, GX, NY)
H_SHAPE = (3, NZ + 1, GX, NY)
PAY_SHAPE = (NB, 2, LANES)
XR_SHAPE, XL_SHAPE = (3 * NZ, NY), (2 * NZ, NY)
UP_SHAPE, DOWN_SHAPE = (2 * NX + GX + 8, NY), (NX + GX + 8, NY)
FIELD = (3, NZ, NX, NY)


def call(kernel, outs, *args, alias=None, name=None, far=(), far_out=(), scratch=()):
    return pl.pallas_call(
        kernel,
        out_shape=[jax.ShapeDtypeStruct(s, F32) for s in outs],
        in_specs=[ANY if k in far else VMEM for k in range(len(args))],
        out_specs=[ANY if k in far_out else VMEM for k in range(len(outs))],
        scratch_shapes=list(scratch),
        input_output_aliases=alias or {},
        name=name,
        compiler_params=pltpu.CompilerParams(vmem_limit_bytes=40 << 20),
    )(*args)


def shifted(value, axis, by):
    devices = lax.axis_size(axis)
    pairs = [(i, i + by) for i in range(devices) if 0 <= i + by < devices]
    return lax.ppermute(value, axis, pairs)


def exchanged(value):
    return lax.all_to_all(value, "fxy", 0, 0, tiled=True)


def iota(shape, dim):
    return lax.broadcasted_iota(jnp.int32, shape, dim)


def column():
    return lax.axis_index("fxy")


def row():
    return lax.axis_index("fz")


def split3(value):
    high = value.astype(BF16)
    rest = value - high.astype(F32)
    middle = rest.astype(BF16)
    low = (rest - middle.astype(F32)).astype(BF16)
    return high, middle, low


def dot3(value, onehot, dims=(((1,), (0,)), ((), ()))):
    rows = value.shape[0]
    parts = jnp.concatenate(split3(value), 0)
    product = lax.dot_general(parts, onehot, dims, preferred_element_type=F32)
    return product[:rows] + (product[rows : 2 * rows] + product[2 * rows :])


def ones_where(condition):
    return jnp.where(condition, 1.0, 0.0).astype(BF16)


def next_y(f):
    rolled = pltpu.roll(f, NY - 1, 1)
    return jnp.where(iota(f.shape, 1) == NY - 1, 0.0, rolled)


def last_y(f):
    rolled = pltpu.roll(f, 1, 1)
    return jnp.where(iota(f.shape, 1) == 0, 0.0, rolled)


def next_x(f):
    return jnp.concatenate([f[1:], f[:1]], 0)


def last_x(f):
    return jnp.concatenate([f[GX - 1 :], f[: GX - 1]], 0)


def copies(pairs, sems):
    started = [pltpu.make_async_copy(a, b, sems.at[k]) for k, (a, b) in enumerate(pairs)]
    for copy in started:
        copy.start()
    return started


def wait(started):
    for copy in started:
        copy.wait()


def lower(got_ref, f):
    lane = iota((8, LANES), 1)
    return jnp.where(lane < HALF, got_ref[0:8, f, :], pltpu.roll(got_ref[8:16, f, :], HALF, 1))


def upper(got_ref, f):
    lane = iota((8, LANES), 1)
    return jnp.where(lane < HALF, pltpu.roll(got_ref[0:8, f, :], HALF, 1), got_ref[8:16, f, :])


def own_ports(cell):
    cell = jnp.concatenate([cell, cell], 1)
    mine = iota((1, LANES), 1) < HALF
    at_row = ones_where((iota((NZ * NX, LANES), 0) == cell // NY) & mine)
    at_y = ones_where(iota((NY, LANES), 0) == cell % NY)
    return at_row, at_y


def at_ports(field, ports):
    at_row, at_y = ports
    return jnp.sum(dot3(field, at_y) * at_row.astype(F32), 0, keepdims=True)


def hist_at(hist, position):
    out = jnp.zeros((1, LANES), F32)
    for k in range(DEPTH + STEPS):
        out = jnp.where(position == k, hist[k : k + 1], out)
    return out


def k_first(
    e_ref, h_ref, cell_ref, node_ref, cond_ref, far_ref, delay_ref, imped_ref, near_hist_ref,
    pay_ref, up_ref, right_ref,
    ez, side, cell, node, cond, far, delay, imped, hist, sems,
):
    pairs = [
        (cell_ref, cell), (node_ref, node), (cond_ref, cond), (e_ref.at[2], ez),
        (far_ref, far), (delay_ref, delay), (imped_ref, imped), (near_hist_ref, hist),
        (h_ref.at[0, NZ - 1], up_ref.at[0:NX]), (h_ref.at[1, NZ - 1], up_ref.at[NX : 2 * NX]),
        (h_ref.at[1:3, :, NX - 8 : NX], side),
    ]
    started = copies(pairs, sems)
    up_ref[2 * NX :] = jnp.zeros((8, NY), F32)
    wait(started[:4])
    here = at_ports(ez[...].reshape(NZ * NX, NY), own_ports(cell[...]))
    first = jnp.concatenate([node[...], cell[...]], 1).astype(F32)
    second = jnp.concatenate([cond[...], here[:, :HALF]], 1)
    pay_ref[...] = jnp.broadcast_to(jnp.concatenate([first, second], 0)[None], PAY_SHAPE)
    wait(started[4:])
    up_ref[2 * NX : 2 * NX + 1, 0:LANES] = far[...].astype(F32)
    up_ref[2 * NX + 1 : 2 * NX + 2, 0:LANES] = delay[...].astype(F32)
    up_ref[2 * NX + 2 : 2 * NX + 3, 0:LANES] = imped[...]
    for k in range(DEPTH):
        up_ref[2 * NX + k : 2 * NX + k + 1, LANES : 2 * LANES] = hist[k]
    for c in range(2):
        for z in range(NZ):
            right_ref[c * NZ + z : c * NZ + z + 1] = side[c, z, 7:8]


def update_e(e_ref, h_ref, d_ref, g_ref):
    for z in range(NZ):
        hx, hy, hz = h_ref[0, z + 1], h_ref[1, z + 1], h_ref[2, z + 1]
        own = hz[:NX]
        curl_x = (own - last_y(own)) - (hy[:NX] - h_ref[1, z, :NX])
        curl_y = (hx[:NX] - h_ref[0, z, :NX]) - (hz - last_x(hz))[:NX]
        curl_z = (hy - last_x(hy))[:NX] - (hx[:NX] - last_y(hx[:NX]))
        d, g = d_ref[z], g_ref[z]
        for c, curl in enumerate((curl_x, curl_y, curl_z)):
            e_ref[c, z + 1, :NX] = d * e_ref[c, z + 1, :NX] + g * curl


def send_x(e_ref, right_ref, left_ref):
    for z in range(NZ):
        for c in range(3):
            right_ref[c * NZ + z : c * NZ + z + 1] = e_ref[c, z + 1, NX - 1 : NX]
        for c in range(2):
            left_ref[c * NZ + z : c * NZ + z + 1] = e_ref[1 + c, z + 1, 0:1]


def own_rows(ref):
    return ref.at[:, 1 : NZ + 1, 0:NX]


def k_start(
    e_in, h_in, d_in, g_in, cell_in, up_ref, right_ref, e_ref, h_ref, pre_ref, xr_ref, xl_ref, d_ref, g_ref, cell_ref, sems
):
    pairs = [(e_in, own_rows(e_ref)), (h_in, own_rows(h_ref)), (d_in, d_ref), (g_in, g_ref), (cell_in, cell_ref)]
    started = copies(pairs, sems)
    first = iota((8, NY), 0)
    for z in range(NZ):
        h_ref[0, z + 1, NX:] = jnp.zeros((8, NY), F32)
        for c in range(2):
            ghost = right_ref[c * NZ + z : c * NZ + z + 1]
            h_ref[1 + c, z + 1, NX:] = jnp.where(first == 7, ghost, 0.0)
    for c in range(3):
        h_ref[c, 0] = jnp.zeros((GX, NY), F32)
        e_ref[c, 0] = jnp.zeros((GX, NY), F32)
        e_ref[c, NZ + 1] = jnp.zeros((GX, NY), F32)
    h_ref[0, 0, :NX] = up_ref[0:NX]
    h_ref[1, 0, :NX] = up_ref[NX : 2 * NX]
    wait(started)
    update_e(e_ref, h_ref, d_ref, g_ref)
    ports = own_ports(cell_ref[...])
    pre = at_ports(e_ref[2, 1 : NZ + 1, :NX].reshape(NZ * NX, NY), ports)
    gain = at_ports(g_ref[...].reshape(NZ * NX, NY), ports)
    pre_ref[...] = jnp.broadcast_to(pre + pltpu.roll(gain, HALF, 1), (8, LANES))
    send_x(e_ref, xr_ref, xl_ref)


def low_onehots(node):
    return [ones_where(iota((LANES, LANES), 0) == node[t : t + 1] % LANES) for t in range(10)]


def own_volts(w, lines, node, inverse_ref):
    high = node // LANES
    sources = jnp.zeros((NB, LANES), F32)
    values = jnp.concatenate([w, lines], 0)
    onehots = low_onehots(node)
    for t in range(10):
        spread = jnp.where(iota((NB, LANES), 0) == high[t : t + 1], values[t : t + 1], 0.0)
        sources = sources + dot3(spread, onehots[t], NT)
    total = jnp.zeros((LANES, LANES), F32)
    for t in range(NB):
        total = total + inverse_ref[0, :, t * LANES : (t + 1) * LANES] * sources[t : t + 1]
    return jnp.sum(total.T, 0, keepdims=True)


def node_values(volts, node):
    high = node // LANES
    rows = []
    onehots = low_onehots(node)
    for t in range(10):
        picked = dot3(volts, onehots[t])
        rows.append(jnp.sum(jnp.where(iota((NB, LANES), 0) == high[t : t + 1], picked, 0.0), 0, keepdims=True))
    return jnp.concatenate(rows, 0)


def line_inputs(state_ref, n):
    own = n - state_ref[STATIC + 4 : STATIC + 5].astype(jnp.int32) + DEPTH
    below = n - state_ref[STATIC + 5 : STATIC + 6].astype(jnp.int32) + DEPTH
    return (
        hist_at(state_ref[FROM_ABOVE : FROM_ABOVE + 16], own),
        hist_at(state_ref[FROM_BELOW : FROM_BELOW + 16], below),
        hist_at(state_ref[OWN : OWN + 16], own),
    )


def next_volts(state_ref, inverse_ref, n):
    into_near, into_below, _ = line_inputs(state_ref, n)
    lines = -jnp.concatenate([into_near, into_below], 0)
    w = state_ref[COND : COND + 8] * state_ref[EZ : EZ + 8]
    return own_volts(w, lines, state_ref[NODE : NODE + 16].astype(jnp.int32), inverse_ref)


def payload(pay_ref, volts, pre):
    pay_ref[...] = jnp.broadcast_to(jnp.concatenate([volts, pre], 0)[None], PAY_SHAPE)


def k_tables(
    got_ref, up_ref, pre_ref, near_in, delay_in, imped_in, near_hist_in, far_hist_in, inverse_in,
    pay_ref, state_ref,
    near_ref, delay_ref, imped_ref, near_hist_ref, far_hist_ref, inverse_ref, sems,
):
    pairs = [
        (near_in, near_ref), (delay_in, delay_ref), (imped_in, imped_ref),
        (near_hist_in, near_hist_ref), (far_hist_in, far_hist_ref), (inverse_in, inverse_ref),
    ]
    started = copies(pairs, sems)
    state_ref[...] = jnp.zeros((ROWS, LANES), F32)
    state_ref[NODE : NODE + 8] = lower(got_ref, 0)
    device = iota((8, LANES), 0) + 8 * (iota((8, LANES), 1) // HALF)
    state_ref[WHERE : WHERE + 8] = upper(got_ref, 0) + (device * (NZ * NX * NY)).astype(F32)
    state_ref[COND : COND + 8] = lower(got_ref, 1)
    state_ref[EZ : EZ + 8] = upper(got_ref, 1)
    far_below = up_ref[2 * NX : 2 * NX + 1, 0:LANES]
    imped_below = jnp.where(row() == 0, 1.0, up_ref[2 * NX + 2 : 2 * NX + 3, 0:LANES])
    wait(started[:5])
    near = near_ref[...].astype(F32)
    static = [near, far_below, imped_ref[...], imped_below, delay_ref[...].astype(F32), up_ref[2 * NX + 1 : 2 * NX + 2, 0:LANES]]
    state_ref[NODE + 8 : NODE + 10] = jnp.concatenate(static[:2], 0)
    state_ref[STATIC : STATIC + 6] = jnp.concatenate(static, 0)
    for k in range(DEPTH):
        back = DEPTH - 1 - k
        state_ref[OWN + k : OWN + k + 1] = near_hist_ref[back]
        state_ref[FROM_ABOVE + k : FROM_ABOVE + k + 1] = far_hist_ref[back]
        state_ref[FROM_BELOW + k : FROM_BELOW + k + 1] = up_ref[2 * NX + back : 2 * NX + back + 1, LANES : 2 * LANES]
    wait(started[5:])
    payload(pay_ref, next_volts(state_ref, inverse_ref, 0), pre_ref[0:1])


def block_row(k):
    block = column() + k
    return jnp.where(block < 0, block + 8, block % 8), block // 8, (block >= 0) & (block < NB)


def spread_currents(e_ref, where, drop):
    row_parts, at_y = [], []
    for k in (-1, 0, 1):
        packed, half, exists = block_row(k)
        pick = iota((8, LANES), 0) == packed
        cell = jnp.sum(jnp.where(pick, where, 0.0), 0, keepdims=True).astype(jnp.int32) % (NZ * NX * NY)
        values = jnp.sum(jnp.where(pick, drop, 0.0), 0, keepdims=True)
        x = (cell // NY) % NX + k * NX
        position = jnp.where((x >= 0) & (x <= NX), x, jnp.where(x == -1, GX - 1, -1))
        inside = (iota((1, LANES), 1) // HALF == half) & exists & (position >= 0)
        target = jnp.where(inside, (cell // (NX * NY)) * GX + position, -1)
        at_row = ones_where(iota((NZ * GX, LANES), 0) == target)
        row_parts.append(jnp.concatenate([at_row * part for part in split3(values)], 0))
        at_y.append(ones_where(iota((NY, LANES), 0) == cell % NY))
    spread = lax.dot_general(jnp.concatenate(row_parts, 1), jnp.concatenate(at_y, 1), NT, preferred_element_type=F32)
    rows = NZ * GX
    spread = spread[:rows] + (spread[rows : 2 * rows] + spread[2 * rows :])
    for z in range(NZ):
        e_ref[2, z + 1] = e_ref[2, z + 1] - spread[z * GX : (z + 1) * GX]


def k_currents(n, last, got_ref, xr_ref, xl_ref, e_in, state_in, e_ref, state_ref, *sends):
    pre = lower(got_ref, 1)
    if n == 0:
        state_ref[GAIN : GAIN + 8] = upper(got_ref, 1)
    at_nodes = node_values(got_ref[:, 0, :], state_ref[NODE : NODE + 16].astype(jnp.int32))
    where = state_ref[WHERE : WHERE + 8]
    current = state_ref[COND : COND + 8] * (state_ref[EZ : EZ + 8] - at_nodes[0:8])
    shared = current
    for k in range(1, LANES):
        same = pltpu.roll(where, k, 1) == where
        shared = shared + jnp.where(same, pltpu.roll(current, k, 1), 0.0)
    gain = state_ref[GAIN : GAIN + 8]
    state_ref[EZ : EZ + 8] = pre - gain * shared

    into_near, into_below, into_own = line_inputs(state_ref, n)
    out_near = -2.0 * at_nodes[8:9] / state_ref[STATIC + 2 : STATIC + 3] - into_near
    out_below = -2.0 * at_nodes[9:10] / state_ref[STATIC + 3 : STATIC + 4] - into_below
    top = jnp.where(row() == NF - 1, -into_own, 0.0)
    state_ref[WAVE : WAVE + 2] = jnp.concatenate([out_near, top], 0)

    first = iota((8, NY), 0)
    for z in range(NZ):
        for c in range(3):
            ghost = jnp.where(first == 7, xr_ref[c * NZ + z : c * NZ + z + 1], 0.0)
            if c:
                ghost = jnp.where(first == 0, xl_ref[(c - 1) * NZ + z : (c - 1) * NZ + z + 1], ghost)
            e_ref[c, z + 1, NX:] = ghost
    spread_currents(e_ref, where, gain * current)

    down_ref = sends[-1]
    down_ref[0:GX] = e_ref[0, 1]
    down_ref[GX : GX + NX] = e_ref[1, 1, :NX]
    down_ref[GX + NX :] = jnp.zeros((8, NY), F32)
    down_ref[GX + NX : GX + NX + 1, 0:LANES] = out_below
    if not last:
        up_ref = sends[0]
        up_ref[0:NX] = e_ref[0, NZ, :NX]
        up_ref[NX : 2 * NX] = e_ref[1, NZ, :NX]
        up_ref[2 * NX : 2 * NX + GX] = e_ref[2, NZ]
        up_ref[2 * NX + GX :] = jnp.zeros((8, NY), F32)
        up_ref[2 * NX + GX : 2 * NX + GX + 1, 0:LANES] = out_near


def new_h(e_ref, h_ref, layer, ex_above, ey_above):
    scale = jnp.where((iota((GX, 1), 0) >= NX) & (column() == 0), 0.0, 0.5)
    ex, ey, ez = e_ref[0, layer], e_ref[1, layer], e_ref[2, layer]
    if layer == 0:
        scale = jnp.where(row() == 0, 0.0, scale)
    hx = h_ref[0, layer] - scale * ((next_y(ez) - ez) - (ey_above - ey))
    hy = h_ref[1, layer] - scale * ((ex_above - ex) - (next_x(ez) - ez))
    hz = h_ref[2, layer] - scale * ((next_x(ey) - ey) - (next_y(ex) - ex))
    return hx, hy, hz


def update_h(e_ref, h_ref, layer):
    for c, value in enumerate(new_h(e_ref, h_ref, layer, e_ref[0, layer + 1], e_ref[1, layer + 1])):
        h_ref[c, layer] = value


def k_inner_h(e_ref, h_in, h_ref):
    for layer in range(1, NZ):
        update_h(e_ref, h_ref, layer)


def k_inner_last(e_ref, h_in, h_ref, e_out, h_out, sems):
    first = copies([(own_rows(e_ref), e_out)], sems)
    for layer in range(1, NZ):
        update_h(e_ref, h_ref, layer)
    second = pltpu.make_async_copy(h_ref.at[:, 1:NZ, 0:NX], h_out.at[:, 0 : NZ - 1], sems.at[1])
    second.start()
    wait(first)
    second.wait()


def k_volts(n, last, up_ref, down_ref, d_ref, g_ref, inverse_ref, cell_ref, e_in, h_in, state_in, e_ref, h_ref, state_ref, pay_ref, xr_ref, xl_ref, *volts_ref):
    at = n - 1 + DEPTH
    wave = down_ref[GX + NX : GX + NX + 1, 0:LANES] + state_ref[WAVE + 1 : WAVE + 2]
    state_ref[OWN + at : OWN + at + 1] = state_ref[WAVE : WAVE + 1]
    state_ref[FROM_ABOVE + at : FROM_ABOVE + at + 1] = wave
    state_ref[FROM_BELOW + at : FROM_BELOW + at + 1] = up_ref[2 * NX + GX : 2 * NX + GX + 1, 0:LANES]
    volts = next_volts(state_ref, inverse_ref, n)
    if last:
        volts_ref[0][...] = volts
    e_ref[0, 0, :NX] = up_ref[0:NX]
    e_ref[1, 0, :NX] = up_ref[NX : 2 * NX]
    e_ref[2, 0] = up_ref[2 * NX : 2 * NX + GX]
    e_ref[0, NZ + 1] = down_ref[0:GX]
    e_ref[1, NZ + 1, :NX] = down_ref[GX : GX + NX]
    update_h(e_ref, h_ref, 0)
    update_h(e_ref, h_ref, NZ)
    update_e(e_ref, h_ref, d_ref, g_ref)
    pre = at_ports(e_ref[2, 1 : NZ + 1, :NX].reshape(NZ * NX, NY), own_ports(cell_ref[...]))
    payload(pay_ref, volts, pre)
    send_x(e_ref, xr_ref, xl_ref)


def k_last(down_ref, state_ref, e_ref, h_ref, h_in, h_out, wave_out, layer_ref, sem):
    ey_above = jnp.concatenate([down_ref[GX : GX + NX], jnp.zeros((8, NY), F32)], 0)
    for c, value in enumerate(new_h(e_ref, h_ref, NZ, down_ref[0:GX], ey_above)):
        layer_ref[c] = value[:NX]
    copy = pltpu.make_async_copy(layer_ref, h_out.at[:, NZ - 1], sem)
    copy.start()
    above = down_ref[GX + NX : GX + NX + 1, 0:LANES] + state_ref[WAVE + 1 : WAVE + 2]
    wave_out[...] = jnp.concatenate([state_ref[WAVE : WAVE + 1], above], 0)[None]
    copy.wait()


def local(
    e_field,
    h_field,
    e_decay,
    e_gain,
    port_cell,
    port_node,
    port_conductance,
    inverse,
    line_near,
    line_far,
    line_delay,
    line_imped,
    hist_near,
    hist_far,
):
    hist_near = jnp.transpose(hist_near, (1, 0, 2))
    hist_far = jnp.transpose(hist_far, (1, 0, 2))
    hist_shape = pltpu.VMEM((DEPTH, 1, LANES), F32)
    line = pltpu.VMEM((1, LANES), F32)
    line_int = pltpu.VMEM((1, LANES), jnp.int32)
    ports_int = pltpu.VMEM((1, HALF), jnp.int32)
    block = pltpu.VMEM((NZ, NX, NY), F32)

    pay, up, right = call(
        k_first,
        [PAY_SHAPE, (2 * NX + 8, NY), (2 * NZ, NY)],
        e_field, h_field, port_cell, port_node, port_conductance, line_far, line_delay, line_imped, hist_near,
        far=range(9),
        scratch=[
            block, pltpu.VMEM((2, NZ, 8, NY), F32), ports_int, ports_int, pltpu.VMEM((1, HALF), F32),
            line_int, line_int, line, hist_shape, pltpu.SemaphoreType.DMA((11,)),
        ],
        name="first",
    )
    got = exchanged(pay)
    up = shifted(up, "fz", 1)
    right = shifted(right, "fxy", 1)
    e, h, pre, xr, xl = call(
        k_start,
        [E_SHAPE, H_SHAPE, (8, LANES), XR_SHAPE, XL_SHAPE],
        e_field, h_field, e_decay, e_gain, port_cell, up, right,
        far=range(5),
        scratch=[block, block, ports_int, pltpu.SemaphoreType.DMA((5,))],
        name="start",
    )
    pay, state = call(
        k_tables,
        [PAY_SHAPE, (ROWS, LANES)],
        got, up, pre, line_near, line_delay, line_imped, hist_near, hist_far, inverse,
        far=range(3, 9),
        scratch=[
            line_int, line_int, line, hist_shape, hist_shape,
            pltpu.VMEM((1, LANES, NB * LANES), F32), pltpu.SemaphoreType.DMA((6,)),
        ],
        name="tables",
    )
    for n in range(STEPS):
        last = n == STEPS - 1
        got = exchanged(pay)
        xr = shifted(xr, "fxy", 1)
        xl = shifted(xl, "fxy", -1)
        e, state, *sends = call(
            functools.partial(k_currents, n, last),
            [E_SHAPE, (ROWS, LANES)] + ([] if last else [UP_SHAPE]) + [DOWN_SHAPE],
            got, xr, xl, e, state,
            alias={3: 0, 4: 1},
            name="currents",
        )
        down = shifted(sends[-1], "fz", -1)
        if last:
            break
        up = shifted(sends[0], "fz", 1)
        (h,) = call(k_inner_h, [H_SHAPE], e, h, alias={1: 0}, name="inner_h")
        e, h, state, pay, xr, xl, *node_volt = call(
            functools.partial(k_volts, n + 1, n + 1 == STEPS - 1),
            [E_SHAPE, H_SHAPE, (ROWS, LANES), PAY_SHAPE, XR_SHAPE, XL_SHAPE] + ([(1, LANES)] if n + 1 == STEPS - 1 else []),
            up, down, e_decay, e_gain, inverse, port_cell, e, h, state,
            alias={6: 0, 7: 1, 8: 2},
            name="volts",
        )
    h, e_out, h_out = call(
        k_inner_last,
        [H_SHAPE, FIELD, FIELD],
        e, h,
        alias={1: 0},
        far_out=(1, 2),
        scratch=[pltpu.SemaphoreType.DMA((2,))],
        name="inner_last",
    )
    h_out, line_wave = call(
        k_last,
        [FIELD, (1, 2, LANES)],
        down, state, e, h, h_out,
        alias={4: 0},
        far=(4,),
        far_out=(0,),
        scratch=[pltpu.VMEM((3, NX, NY), F32), pltpu.SemaphoreType.DMA],
        name="last",
    )
    return e_out, h_out, node_volt[0], line_wave


def solution(mesh):
    placed = (
        P(None, "fz", "fxy", None),
        P(None, "fz", "fxy", None),
        P("fz", "fxy", None),
        P("fz", "fxy", None),
        P("fz", "fxy"),
        P("fz", "fxy"),
        P("fz", "fxy"),
        P("fz", "fxy", None),
        P("fz", None),
        P("fz", None),
        P("fz", None),
        P("fz", None),
        P("fz", None, None),
        P("fz", None, None),
    )
    return jax.shard_map(
        local,
        mesh=mesh,
        in_specs=placed,
        out_specs=(
            P(None, "fz", "fxy", None),
            P(None, "fz", "fxy", None),
            P("fz", "fxy"),
            P("fz", None, None),
        ),
        check_vma=False,
    )
```

```python
import functools

import jax
import jax.numpy as jnp
from jax import lax
from jax.experimental import pallas as pl
from jax.experimental.pallas import tpu as pltpu
from jax.sharding import PartitionSpec as P

STEPS = 4
F32 = jnp.float32
BF16 = jnp.bfloat16
NZ = 8
NX = 16
NY = 512
GX = 24
DEEP = 4
NF = 32
NB = 16
HALF = 64
LANES = 128
DEPTH = 6
VMEM = pl.BlockSpec(memory_space=pltpu.VMEM)
ANY = pl.BlockSpec(memory_space=pltpu.HBM)
NT = (((1,), (1,)), ((), ()))
NODE, WHERE, COND, GAIN, EZ, STATIC, OWN, FROM_ABOVE, FROM_BELOW, WAVE, ROWS = 0, 16, 24, 32, 40, 48, 56, 72, 88, 104, 112
E_SHAPE = (3, NZ + 2, GX, NY)
H_SHAPE = (3, NZ + 1, GX, NY)
PAY_SHAPE = (NB, 2, LANES)
LAYERS = 8 * NZ + 2
SIDE_SHAPE = (LAYERS * DEEP, NY)
WIDE = (NZ, GX, NY)
UP_SHAPE, DOWN_SHAPE = (3 * GX + 8, NY), (2 * GX + 8, NY)
FIELD = (3, NZ, NX, NY)


def call(kernel, outs, *args, alias=None, name=None, far=(), far_out=(), scratch=(), room=40 << 20):
    return pl.pallas_call(
        kernel,
        out_shape=[jax.ShapeDtypeStruct(s, F32) for s in outs],
        in_specs=[ANY if k in far else VMEM for k in range(len(args))],
        out_specs=[ANY if k in far_out else VMEM for k in range(len(outs))],
        scratch_shapes=list(scratch),
        input_output_aliases=alias or {},
        name=name,
        compiler_params=pltpu.CompilerParams(vmem_limit_bytes=room),
    )(*args)


def shifted(value, axis, by):
    devices = lax.axis_size(axis)
    pairs = [(i, i + by) for i in range(devices) if 0 <= i + by < devices]
    return lax.ppermute(value, axis, pairs)


def exchanged(value):
    return lax.all_to_all(value, "fxy", 0, 0, tiled=True)


def iota(shape, dim):
    return lax.broadcasted_iota(jnp.int32, shape, dim)


def column():
    return lax.axis_index("fxy")


def row():
    return lax.axis_index("fz")


def split3(value):
    high = value.astype(BF16)
    rest = value - high.astype(F32)
    middle = rest.astype(BF16)
    low = (rest - middle.astype(F32)).astype(BF16)
    return high, middle, low


def dot3(value, onehot, dims=(((1,), (0,)), ((), ()))):
    rows = value.shape[0]
    parts = jnp.concatenate(split3(value), 0)
    product = lax.dot_general(parts, onehot, dims, preferred_element_type=F32)
    return product[:rows] + (product[rows : 2 * rows] + product[2 * rows :])


def ones_where(condition):
    return jnp.where(condition, 1.0, 0.0).astype(BF16)


def next_y(f):
    rolled = pltpu.roll(f, NY - 1, 1)
    return jnp.where(iota(f.shape, 1) == NY - 1, 0.0, rolled)


def last_y(f):
    rolled = pltpu.roll(f, 1, 1)
    return jnp.where(iota(f.shape, 1) == 0, 0.0, rolled)


def next_x(f):
    return jnp.concatenate([f[1:], f[:1]], 0)


def last_x(f):
    return jnp.concatenate([f[GX - 1 :], f[: GX - 1]], 0)


def copies(pairs, sems):
    started = [pltpu.make_async_copy(a, b, sems.at[k]) for k, (a, b) in enumerate(pairs)]
    for copy in started:
        copy.start()
    return started


def wait(started):
    for copy in started:
        copy.wait()


def lower(got_ref, f):
    lane = iota((8, LANES), 1)
    return jnp.where(lane < HALF, got_ref[0:8, f, :], pltpu.roll(got_ref[8:16, f, :], HALF, 1))


def upper(got_ref, f):
    lane = iota((8, LANES), 1)
    return jnp.where(lane < HALF, pltpu.roll(got_ref[0:8, f, :], HALF, 1), got_ref[8:16, f, :])


def own_ports(cell):
    cell = jnp.concatenate([cell, cell], 1)
    mine = iota((1, LANES), 1) < HALF
    at_row = ones_where((iota((NZ * NX, LANES), 0) == cell // NY) & mine)
    at_y = ones_where(iota((NY, LANES), 0) == cell % NY)
    return at_row, at_y


def at_ports(field, ports):
    at_row, at_y = ports
    return jnp.sum(dot3(field, at_y) * at_row.astype(F32), 0, keepdims=True)


def hist_at(hist, position):
    out = jnp.zeros((1, LANES), F32)
    for k in range(DEPTH + STEPS):
        out = jnp.where(position == k, hist[k : k + 1], out)
    return out


def k_first(
    e_ref, h_ref, cell_ref, node_ref, cond_ref, far_ref, delay_ref, imped_ref, near_hist_ref,
    pay_out, up_ref, right_ref,
    ez, side, cell, node, cond, far, delay, imped, hist, pay_ref, sems,
):
    pairs = [
        (cell_ref, cell), (node_ref, node), (cond_ref, cond), (e_ref.at[2], ez),
        (far_ref, far), (delay_ref, delay), (imped_ref, imped), (near_hist_ref, hist),
        (h_ref.at[0, NZ - 1], up_ref.at[0:NX]), (h_ref.at[1, NZ - 1], up_ref.at[NX : 2 * NX]),
        (h_ref.at[1:3, :, NX - 8 : NX], side),
    ]
    started = copies(pairs, sems)
    up_ref[2 * NX :] = jnp.zeros((8, NY), F32)
    wait(started[:4])
    here = at_ports(ez[...].reshape(NZ * NX, NY), own_ports(cell[...]))
    first = jnp.concatenate([node[...], cell[...]], 1).astype(F32)
    second = jnp.concatenate([cond[...], here[:, :HALF]], 1)
    sending = payload(pay_out, pay_ref, sems.at[11], first, second)
    wait(started[4:])
    up_ref[2 * NX : 2 * NX + 1, 0:LANES] = far[...].astype(F32)
    up_ref[2 * NX + 1 : 2 * NX + 2, 0:LANES] = delay[...].astype(F32)
    up_ref[2 * NX + 2 : 2 * NX + 3, 0:LANES] = imped[...]
    for k in range(DEPTH):
        up_ref[2 * NX + k : 2 * NX + k + 1, LANES : 2 * LANES] = hist[k]
    for c in range(2):
        for z in range(NZ):
            right_ref[c * NZ + z : c * NZ + z + 1] = side[c, z, 7:8]
    sending.wait()


def update_e(e_ref, h_ref, d_ref, g_ref, components, width):
    for z in range(NZ):
        hx, hy, hz = h_ref[0, z + 1], h_ref[1, z + 1], h_ref[2, z + 1]
        d, g = d_ref[z], g_ref[z]
        for c in components:
            if c == 0:
                own = hz[:width]
                curl = (own - last_y(own)) - (hy[:width] - h_ref[1, z, :width])
            elif c == 1:
                curl = (hx[:width] - h_ref[0, z, :width]) - (hz - last_x(hz))[:width]
            else:
                own = hx[:width]
                curl = (hy - last_x(hy))[:width] - (own - last_y(own))
            e_ref[c, z + 1, :width] = d * e_ref[c, z + 1, :width] + g * curl


def own_rows(ref):
    return ref.at[:, 1 : NZ + 1, 0:NX]


def k_start(
    e_in, h_in, d_in, g_in, cell_in, up_ref, right_ref, e_ref, h_ref, pre_ref, right_out, left_out,
    d_ref, g_ref, cell_ref, send_right, send_left, sems,
):
    pairs = [(e_in, own_rows(e_ref)), (h_in, own_rows(h_ref)), (d_in, d_ref), (g_in, g_ref), (cell_in, cell_ref)]
    started = copies(pairs, sems)
    first = iota((8, NY), 0)
    for z in range(NZ):
        h_ref[0, z + 1, NX:] = jnp.zeros((8, NY), F32)
        for c in range(2):
            ghost = right_ref[c * NZ + z : c * NZ + z + 1]
            h_ref[1 + c, z + 1, NX:] = jnp.where(first == 7, ghost, 0.0)
    for c in range(3):
        h_ref[c, 0] = jnp.zeros((GX, NY), F32)
        e_ref[c, 0] = jnp.zeros((GX, NY), F32)
        e_ref[c, NZ + 1] = jnp.zeros((GX, NY), F32)
    h_ref[0, 0, :NX] = up_ref[0:NX]
    h_ref[1, 0, :NX] = up_ref[NX : 2 * NX]
    wait(started)
    update_e(e_ref, h_ref, d_ref, g_ref, (0, 1, 2), NX)
    layers = [(e_ref, (c, z + 1)) for c in range(3) for z in range(NZ)]
    layers += [(h_ref, (c, z + 1)) for c in range(3) for z in range(NZ)] + [(h_ref, (c, 0)) for c in range(2)]
    layers += [(d_ref, (z,)) for z in range(NZ)] + [(g_ref, (z,)) for z in range(NZ)]
    for k, (ref, at) in enumerate(layers):
        send_right[k * DEEP : (k + 1) * DEEP] = ref[(*at, slice(NX - DEEP, NX))]
        send_left[k * DEEP : (k + 1) * DEEP] = ref[(*at, slice(0, DEEP))]
    started = copies([(send_right, right_out), (send_left, left_out)], sems)
    ports = own_ports(cell_ref[...])
    pre = at_ports(e_ref[2, 1 : NZ + 1, :NX].reshape(NZ * NX, NY), ports)
    gain = at_ports(g_ref[...].reshape(NZ * NX, NY), ports)
    pre_ref[...] = jnp.broadcast_to(pre + pltpu.roll(gain, HALF, 1), (8, LANES))
    wait(started)


def k_widen(right_in, left_in, d_in, g_in, e_in, h_in, e_ref, h_ref, d_out, g_out, right_ref, left_ref, d_tile, g_tile, sems):
    pairs = [(right_in, right_ref), (left_in, left_ref), (d_in, d_out.at[:, 0:NX]), (g_in, g_out.at[:, 0:NX])]
    started = copies(pairs, sems)
    wait(started[:2])

    def tile(k):
        rows = slice(k * DEEP, (k + 1) * DEEP)
        return jnp.concatenate([left_ref[rows], right_ref[rows]], 0)

    for z in range(NZ):
        d_tile[z] = tile(6 * NZ + 2 + z)
        g_tile[z] = tile(7 * NZ + 2 + z)
    more = [pltpu.make_async_copy(d_tile, d_out.at[:, NX:], sems.at[4]), pltpu.make_async_copy(g_tile, g_out.at[:, NX:], sems.at[5])]
    for copy in more:
        copy.start()
    for c in range(3):
        for z in range(NZ):
            e_ref[c, z + 1, NX:] = tile(c * NZ + z)
            h_ref[c, z + 1, NX:] = tile(3 * NZ + c * NZ + z)
    for c in range(2):
        h_ref[c, 0, NX:] = tile(6 * NZ + c)
    wait(started[2:])
    wait(more)


def low_onehots(node):
    return [ones_where(iota((LANES, LANES), 0) == node[t : t + 1] % LANES) for t in range(10)]


def own_volts(w, lines, node, inverse_ref):
    high = node // LANES
    sources = jnp.zeros((NB, LANES), F32)
    values = jnp.concatenate([w, lines], 0)
    onehots = low_onehots(node)
    for t in range(10):
        spread = jnp.where(iota((NB, LANES), 0) == high[t : t + 1], values[t : t + 1], 0.0)
        sources = sources + dot3(spread, onehots[t], NT)
    total = jnp.zeros((LANES, LANES), F32)
    for t in range(NB):
        total = total + inverse_ref[0, :, t * LANES : (t + 1) * LANES] * sources[t : t + 1]
    return jnp.sum(total.T, 0, keepdims=True)


def node_values(volts, node):
    high = node // LANES
    rows = []
    onehots = low_onehots(node)
    for t in range(10):
        picked = dot3(volts, onehots[t])
        rows.append(jnp.sum(jnp.where(iota((NB, LANES), 0) == high[t : t + 1], picked, 0.0), 0, keepdims=True))
    return jnp.concatenate(rows, 0)


def line_inputs(state_ref, n):
    own = n - state_ref[STATIC + 4 : STATIC + 5].astype(jnp.int32) + DEPTH
    below = n - state_ref[STATIC + 5 : STATIC + 6].astype(jnp.int32) + DEPTH
    return (
        hist_at(state_ref[FROM_ABOVE : FROM_ABOVE + 16], own),
        hist_at(state_ref[FROM_BELOW : FROM_BELOW + 16], below),
        hist_at(state_ref[OWN : OWN + 16], own),
    )


def next_volts(state_ref, inverse_ref, n):
    into_near, into_below, _ = line_inputs(state_ref, n)
    lines = -jnp.concatenate([into_near, into_below], 0)
    w = state_ref[COND : COND + 8] * state_ref[EZ : EZ + 8]
    return own_volts(w, lines, state_ref[NODE : NODE + 16].astype(jnp.int32), inverse_ref)


def payload(pay_out, pay_ref, sem, volts, pre):
    pay_ref[...] = jnp.broadcast_to(jnp.concatenate([volts, pre], 0)[None], PAY_SHAPE)
    copy = pltpu.make_async_copy(pay_ref, pay_out, sem)
    copy.start()
    return copy


def k_tables(
    got_ref, up_ref, pre_ref, near_in, delay_in, imped_in, near_hist_in, far_hist_in, inverse_in,
    pay_out, state_ref,
    near_ref, delay_ref, imped_ref, near_hist_ref, far_hist_ref, inverse_ref, pay_ref, sems,
):
    pairs = [
        (near_in, near_ref), (delay_in, delay_ref), (imped_in, imped_ref),
        (near_hist_in, near_hist_ref), (far_hist_in, far_hist_ref), (inverse_in, inverse_ref),
    ]
    started = copies(pairs, sems)
    state_ref[...] = jnp.zeros((ROWS, LANES), F32)
    state_ref[NODE : NODE + 8] = lower(got_ref, 0)
    device = iota((8, LANES), 0) + 8 * (iota((8, LANES), 1) // HALF)
    state_ref[WHERE : WHERE + 8] = upper(got_ref, 0) + (device * (NZ * NX * NY)).astype(F32)
    state_ref[COND : COND + 8] = lower(got_ref, 1)
    state_ref[EZ : EZ + 8] = upper(got_ref, 1)
    far_below = up_ref[2 * NX : 2 * NX + 1, 0:LANES]
    imped_below = jnp.where(row() == 0, 1.0, up_ref[2 * NX + 2 : 2 * NX + 3, 0:LANES])
    wait(started[:5])
    near = near_ref[...].astype(F32)
    static = [near, far_below, imped_ref[...], imped_below, delay_ref[...].astype(F32), up_ref[2 * NX + 1 : 2 * NX + 2, 0:LANES]]
    state_ref[NODE + 8 : NODE + 10] = jnp.concatenate(static[:2], 0)
    state_ref[STATIC : STATIC + 6] = jnp.concatenate(static, 0)
    for k in range(DEPTH):
        back = DEPTH - 1 - k
        state_ref[OWN + k : OWN + k + 1] = near_hist_ref[back]
        state_ref[FROM_ABOVE + k : FROM_ABOVE + k + 1] = far_hist_ref[back]
        state_ref[FROM_BELOW + k : FROM_BELOW + k + 1] = up_ref[2 * NX + back : 2 * NX + back + 1, LANES : 2 * LANES]
    wait(started[5:])
    payload(pay_out, pay_ref, sems.at[6], next_volts(state_ref, inverse_ref, 0), pre_ref[0:1]).wait()


def block_row(k):
    block = column() + k
    return jnp.where(block < 0, block + 8, block % 8), block // 8, (block >= 0) & (block < NB)


def spread_currents(e_ref, where, drop):
    row_parts, at_y = [], []
    for k in (-1, 0, 1):
        packed, half, exists = block_row(k)
        pick = iota((8, LANES), 0) == packed
        cell = jnp.sum(jnp.where(pick, where, 0.0), 0, keepdims=True).astype(jnp.int32) % (NZ * NX * NY)
        values = jnp.sum(jnp.where(pick, drop, 0.0), 0, keepdims=True)
        x = (cell // NY) % NX + k * NX
        position = jnp.where((x >= 0) & (x < NX + DEEP), x, jnp.where((x < 0) & (x >= -DEEP), x + GX, -1))
        inside = (iota((1, LANES), 1) // HALF == half) & exists & (position >= 0)
        target = jnp.where(inside, (cell // (NX * NY)) * GX + position, -1)
        at_row = ones_where(iota((NZ * GX, LANES), 0) == target)
        row_parts.append(jnp.concatenate([at_row * part for part in split3(values)], 0))
        at_y.append(ones_where(iota((NY, LANES), 0) == cell % NY))
    spread = lax.dot_general(jnp.concatenate(row_parts, 1), jnp.concatenate(at_y, 1), NT, preferred_element_type=F32)
    rows = NZ * GX
    spread = spread[:rows] + (spread[rows : 2 * rows] + spread[2 * rows :])
    for z in range(NZ):
        e_ref[2, z + 1] = e_ref[2, z + 1] - spread[z * GX : (z + 1) * GX]


def k_currents(n, last, got_ref, e_in, state_in, e_ref, state_ref, *sends):
    pre = lower(got_ref, 1)
    if n == 0:
        state_ref[GAIN : GAIN + 8] = upper(got_ref, 1)
    at_nodes = node_values(got_ref[:, 0, :], state_ref[NODE : NODE + 16].astype(jnp.int32))
    where = state_ref[WHERE : WHERE + 8]
    current = state_ref[COND : COND + 8] * (state_ref[EZ : EZ + 8] - at_nodes[0:8])
    shared = current
    for k in range(1, LANES):
        same = pltpu.roll(where, k, 1) == where
        shared = shared + jnp.where(same, pltpu.roll(current, k, 1), 0.0)
    gain = state_ref[GAIN : GAIN + 8]
    state_ref[EZ : EZ + 8] = pre - gain * shared

    into_near, into_below, into_own = line_inputs(state_ref, n)
    out_near = -2.0 * at_nodes[8:9] / state_ref[STATIC + 2 : STATIC + 3] - into_near
    out_below = -2.0 * at_nodes[9:10] / state_ref[STATIC + 3 : STATIC + 4] - into_below
    top = jnp.where(row() == NF - 1, -into_own, 0.0)
    state_ref[WAVE : WAVE + 2] = jnp.concatenate([out_near, top], 0)

    spread_currents(e_ref, where, gain * current)

    down_ref = sends[-1]
    for c in range(2):
        down_ref[c * GX : (c + 1) * GX] = e_ref[c, 1]
    down_ref[2 * GX :] = jnp.zeros((8, NY), F32)
    down_ref[2 * GX : 2 * GX + 1, 0:LANES] = out_below
    if not last:
        up_ref = sends[0]
        for c in range(3):
            up_ref[c * GX : (c + 1) * GX] = e_ref[c, NZ]
        up_ref[3 * GX :] = jnp.zeros((8, NY), F32)
        up_ref[3 * GX : 3 * GX + 1, 0:LANES] = out_near


def new_h(e_ref, h_ref, layer, ex_above, ey_above):
    scale = jnp.where((iota((GX, 1), 0) >= GX - DEEP) & (column() == 0), 0.0, 0.5)
    ex, ey, ez = e_ref[0, layer], e_ref[1, layer], e_ref[2, layer]
    if layer == 0:
        scale = jnp.where(row() == 0, 0.0, scale)
    hx = h_ref[0, layer] - scale * ((next_y(ez) - ez) - (ey_above - ey))
    hy = h_ref[1, layer] - scale * ((ex_above - ex) - (next_x(ez) - ez))
    hz = h_ref[2, layer] - scale * ((next_x(ey) - ey) - (next_y(ex) - ex))
    return hx, hy, hz


def update_h(e_ref, h_ref, layer):
    for c, value in enumerate(new_h(e_ref, h_ref, layer, e_ref[0, layer + 1], e_ref[1, layer + 1])):
        h_ref[c, layer] = value


def k_inner_h(e_ref, h_in, h_ref):
    for layer in range(1, NZ):
        update_h(e_ref, h_ref, layer)


def k_inner_last(e_ref, h_in, h_ref, e_out, h_out, sems):
    first = copies([(own_rows(e_ref), e_out)], sems)
    for layer in range(1, NZ):
        update_h(e_ref, h_ref, layer)
    second = pltpu.make_async_copy(h_ref.at[:, 1:NZ, 0:NX], h_out.at[:, 0 : NZ - 1], sems.at[1])
    second.start()
    wait(first)
    second.wait()


def k_volts(
    n, last, up_ref, down_ref, d_ref, g_ref, inverse_ref, cell_ref, e_in, h_in, state_in,
    e_ref, h_ref, state_ref, pay_out, *rest,
):
    pay_ref, sem = rest[-2:]
    at = n - 1 + DEPTH
    state_ref[OWN + at : OWN + at + 1] = state_ref[WAVE : WAVE + 1]
    state_ref[FROM_ABOVE + at : FROM_ABOVE + at + 1] = down_ref[2 * GX : 2 * GX + 1, 0:LANES] + state_ref[WAVE + 1 : WAVE + 2]
    state_ref[FROM_BELOW + at : FROM_BELOW + at + 1] = up_ref[3 * GX : 3 * GX + 1, 0:LANES]
    volts = next_volts(state_ref, inverse_ref, n)
    if last:
        rest[0][...] = volts
    for c in range(3):
        e_ref[c, 0] = up_ref[c * GX : (c + 1) * GX]
    for c in range(2):
        e_ref[c, NZ + 1] = down_ref[c * GX : (c + 1) * GX]
    update_h(e_ref, h_ref, 0)
    update_h(e_ref, h_ref, NZ)
    update_e(e_ref, h_ref, d_ref, g_ref, (2,), GX)
    pre = at_ports(e_ref[2, 1 : NZ + 1, :NX].reshape(NZ * NX, NY), own_ports(cell_ref[...]))
    payload(pay_out, pay_ref, sem, volts, pre).wait()


def k_exy(h_ref, d_ref, g_ref, e_in, e_ref):
    update_e(e_ref, h_ref, d_ref, g_ref, (0, 1), GX)


def k_last(down_ref, state_ref, e_ref, h_ref, h_in, h_out, wave_out, layer_ref, sem):
    for c, value in enumerate(new_h(e_ref, h_ref, NZ, down_ref[0:GX], down_ref[GX : 2 * GX])):
        layer_ref[c] = value[:NX]
    copy = pltpu.make_async_copy(layer_ref, h_out.at[:, NZ - 1], sem)
    copy.start()
    above = down_ref[2 * GX : 2 * GX + 1, 0:LANES] + state_ref[WAVE + 1 : WAVE + 2]
    wave_out[...] = jnp.concatenate([state_ref[WAVE : WAVE + 1], above], 0)[None]
    copy.wait()


def local(
    e_field,
    h_field,
    e_decay,
    e_gain,
    port_cell,
    port_node,
    port_conductance,
    inverse,
    line_near,
    line_far,
    line_delay,
    line_imped,
    hist_near,
    hist_far,
):
    hist_near = jnp.transpose(hist_near, (1, 0, 2))
    hist_far = jnp.transpose(hist_far, (1, 0, 2))
    hist_shape = pltpu.VMEM((DEPTH, 1, LANES), F32)
    line = pltpu.VMEM((1, LANES), F32)
    line_int = pltpu.VMEM((1, LANES), jnp.int32)
    ports_int = pltpu.VMEM((1, HALF), jnp.int32)
    block = pltpu.VMEM((NZ, NX, NY), F32)
    pay_scratch = pltpu.VMEM(PAY_SHAPE, F32)
    side = pltpu.VMEM(SIDE_SHAPE, F32)
    tiles = pltpu.VMEM((NZ, 8, NY), F32)

    pay, up, right = call(
        k_first,
        [PAY_SHAPE, (2 * NX + 8, NY), (2 * NZ, NY)],
        e_field, h_field, port_cell, port_node, port_conductance, line_far, line_delay, line_imped, hist_near,
        far=range(9),
        scratch=[
            block, pltpu.VMEM((2, NZ, 8, NY), F32), ports_int, ports_int, pltpu.VMEM((1, HALF), F32),
            line_int, line_int, line, hist_shape, pay_scratch, pltpu.SemaphoreType.DMA((12,)),
        ],
        far_out=(0,),
        room=67000000,
        name="first",
    )
    got = exchanged(pay)
    up = shifted(up, "fz", 1)
    right = shifted(right, "fxy", 1)
    e, h, pre, to_right, to_left = call(
        k_start,
        [E_SHAPE, H_SHAPE, (8, LANES), SIDE_SHAPE, SIDE_SHAPE],
        e_field, h_field, e_decay, e_gain, port_cell, up, right,
        far=range(5),
        far_out=(3, 4),
        scratch=[block, block, ports_int, side, side, pltpu.SemaphoreType.DMA((5,))],
        name="start",
    )
    pay, state = call(
        k_tables,
        [PAY_SHAPE, (ROWS, LANES)],
        got, up, pre, line_near, line_delay, line_imped, hist_near, hist_far, inverse,
        far=range(3, 9),
        scratch=[
            line_int, line_int, line, hist_shape, hist_shape,
            pltpu.VMEM((1, LANES, NB * LANES), F32), pay_scratch, pltpu.SemaphoreType.DMA((7,)),
        ],
        far_out=(0,),
        name="tables",
    )
    to_right, to_left, pay = lax.optimization_barrier((to_right, to_left, pay))
    for n in range(STEPS):
        last = n == STEPS - 1
        got = exchanged(pay)
        if n == 0:
            e, h, d, g = call(
                k_widen,
                [E_SHAPE, H_SHAPE, WIDE, WIDE],
                shifted(to_right, "fxy", 1), shifted(to_left, "fxy", -1), e_decay, e_gain, e, h,
                far=range(4),
                far_out=(2, 3),
                alias={4: 0, 5: 1},
                scratch=[side, side, tiles, tiles, pltpu.SemaphoreType.DMA((6,))],
                name="widen",
            )
        else:
            (e,) = call(k_exy, [E_SHAPE], h, d, g, e, alias={3: 0}, name="exy")
        e, state, *sends = call(
            functools.partial(k_currents, n, last),
            [E_SHAPE, (ROWS, LANES)] + ([] if last else [UP_SHAPE]) + [DOWN_SHAPE],
            got, e, state,
            alias={1: 0, 2: 1},
            name="currents",
        )
        down = shifted(sends[-1], "fz", -1)
        if last:
            break
        up = shifted(sends[0], "fz", 1)
        (h,) = call(k_inner_h, [H_SHAPE], e, h, alias={1: 0}, name="inner_h")
        e, h, state, pay, *node_volt = call(
            functools.partial(k_volts, n + 1, n + 1 == STEPS - 1),
            [E_SHAPE, H_SHAPE, (ROWS, LANES), PAY_SHAPE] + ([(1, LANES)] if n + 1 == STEPS - 1 else []),
            up, down, d, g, inverse, port_cell, e, h, state,
            alias={6: 0, 7: 1, 8: 2},
            far_out=(3,),
            scratch=[pay_scratch, pltpu.SemaphoreType.DMA],
            name="volts",
        )
    h, e_out, h_out = call(
        k_inner_last,
        [H_SHAPE, FIELD, FIELD],
        e, h,
        alias={1: 0},
        far_out=(1, 2),
        scratch=[pltpu.SemaphoreType.DMA((2,))],
        name="inner_last",
    )
    h_out, line_wave = call(
        k_last,
        [FIELD, (1, 2, LANES)],
        down, state, e, h, h_out,
        alias={4: 0},
        far=(4,),
        far_out=(0,),
        scratch=[pltpu.VMEM((3, NX, NY), F32), pltpu.SemaphoreType.DMA],
        name="last",
    )
    return e_out, h_out, node_volt[0], line_wave


def solution(mesh):
    placed = (
        P(None, "fz", "fxy", None),
        P(None, "fz", "fxy", None),
        P("fz", "fxy", None),
        P("fz", "fxy", None),
        P("fz", "fxy"),
        P("fz", "fxy"),
        P("fz", "fxy"),
        P("fz", "fxy", None),
        P("fz", None),
        P("fz", None),
        P("fz", None),
        P("fz", None),
        P("fz", None, None),
        P("fz", None, None),
    )
    return jax.shard_map(
        local,
        mesh=mesh,
        in_specs=placed,
        out_specs=(
            P(None, "fz", "fxy", None),
            P(None, "fz", "fxy", None),
            P("fz", "fxy"),
            P("fz", None, None),
        ),
        check_vma=False,
    )
```

```python
import functools

import jax
import jax.numpy as jnp
from jax import lax
from jax.experimental import pallas as pl
from jax.experimental.pallas import tpu as pltpu
from jax.sharding import PartitionSpec as P

STEPS = 4
F32 = jnp.float32
BF16 = jnp.bfloat16
NZ = 8
NX = 16
NY = 512
GX = 24
DEEP = 4
NF = 32
NB = 16
HALF = 64
LANES = 128
DEPTH = 6
VMEM = pl.BlockSpec(memory_space=pltpu.VMEM)
ANY = pl.BlockSpec(memory_space=pltpu.HBM)
NT = (((1,), (1,)), ((), ()))
NODE, WHERE, COND, GAIN, EZ, STATIC, OWN, FROM_ABOVE, FROM_BELOW, WAVE, ROWS = 0, 16, 24, 32, 40, 48, 56, 72, 88, 104, 112
E_SHAPE = (3, NZ + 2, GX, NY)
H_SHAPE = (3, NZ + 1, GX, NY)
PAY_SHAPE = (NB, 2, LANES)
LAYERS = 8 * NZ
SIDE_SHAPE = (LAYERS * DEEP, NY)
WIDE = (NZ, GX, NY)
UP_SHAPE, DOWN_SHAPE, TOP_SHAPE = (3 * GX + 8, NY), (2 * GX + 8, NY), (2 * GX, NY)
LINES_SHAPE = (8, 2 * LANES)
FIELD = (3, NZ, NX, NY)


def call(kernel, outs, *args, alias=None, name=None, far=(), far_out=(), scratch=(), room=40 << 20):
    args = [pltpu.with_memory_space_constraint(x, pltpu.HBM) if k in far else x for k, x in enumerate(args)]
    return pl.pallas_call(
        kernel,
        out_shape=[pltpu.HBM(s, F32) if k in far_out else jax.ShapeDtypeStruct(s, F32) for k, s in enumerate(outs)],
        in_specs=[ANY if k in far else VMEM for k in range(len(args))],
        out_specs=[ANY if k in far_out else VMEM for k in range(len(outs))],
        scratch_shapes=list(scratch),
        input_output_aliases=alias or {},
        name=name,
        compiler_params=pltpu.CompilerParams(vmem_limit_bytes=room),
    )(*args)


def shifted(value, axis, by):
    devices = lax.axis_size(axis)
    pairs = [(i, i + by) for i in range(devices) if 0 <= i + by < devices]
    return lax.ppermute(value, axis, pairs)


def exchanged(value):
    return lax.all_to_all(value, "fxy", 0, 0, tiled=True)


def iota(shape, dim):
    return lax.broadcasted_iota(jnp.int32, shape, dim)


def column():
    return lax.axis_index("fxy")


def row():
    return lax.axis_index("fz")


def split3(value):
    high = value.astype(BF16)
    rest = value - high.astype(F32)
    middle = rest.astype(BF16)
    low = (rest - middle.astype(F32)).astype(BF16)
    return high, middle, low


def dot3(value, onehot, dims=(((1,), (0,)), ((), ()))):
    rows = value.shape[0]
    parts = jnp.concatenate(split3(value), 0)
    product = lax.dot_general(parts, onehot, dims, preferred_element_type=F32)
    return product[:rows] + (product[rows : 2 * rows] + product[2 * rows :])


def ones_where(condition):
    return jnp.where(condition, 1.0, 0.0).astype(BF16)


def next_y(f):
    rolled = pltpu.roll(f, NY - 1, 1)
    return jnp.where(iota(f.shape, 1) == NY - 1, 0.0, rolled)


def last_y(f):
    rolled = pltpu.roll(f, 1, 1)
    return jnp.where(iota(f.shape, 1) == 0, 0.0, rolled)


def next_x(f):
    return jnp.concatenate([f[1:], f[:1]], 0)


def last_x(f):
    return jnp.concatenate([f[GX - 1 :], f[: GX - 1]], 0)


def copies(pairs, sems):
    started = [pltpu.make_async_copy(a, b, sems.at[k]) for k, (a, b) in enumerate(pairs)]
    for copy in started:
        copy.start()
    return started


def wait(started):
    for copy in started:
        copy.wait()


def lower(got_ref, f):
    lane = iota((8, LANES), 1)
    return jnp.where(lane < HALF, got_ref[0:8, f, :], pltpu.roll(got_ref[8:16, f, :], HALF, 1))


def upper(got_ref, f):
    lane = iota((8, LANES), 1)
    return jnp.where(lane < HALF, pltpu.roll(got_ref[0:8, f, :], HALF, 1), got_ref[8:16, f, :])


def own_ports(cell):
    cell = jnp.concatenate([cell, cell], 1)
    mine = iota((1, LANES), 1) < HALF
    at_row = ones_where((iota((NZ * NX, LANES), 0) == cell // NY) & mine)
    at_y = ones_where(iota((NY, LANES), 0) == cell % NY)
    return at_row, at_y


def at_ports(field, ports):
    at_row, at_y = ports
    return jnp.sum(dot3(field, at_y) * at_row.astype(F32), 0, keepdims=True)


def hist_at(hist, position):
    out = jnp.zeros((1, LANES), F32)
    for k in range(DEPTH + STEPS):
        out = jnp.where(position == k, hist[k : k + 1], out)
    return out


def k_first(
    e_in, h_in, d_in, g_in, cell_ref, node_ref, cond_ref, far_ref, delay_ref, imped_ref, near_hist_ref,
    pay_out, lines_ref, right_out, left_out,
    e_ref, h_ref, d_ref, g_ref, cell, node, cond, far, delay, imped, hist, pay_ref, right_ref, left_ref, sems,
):
    pairs = [
        (cell_ref, cell), (node_ref, node), (cond_ref, cond), (e_in.at[2], e_ref.at[2]),
        (e_in.at[0:2], e_ref.at[0:2]), (h_in, h_ref), (d_in, d_ref), (g_in, g_ref),
        (far_ref, far), (delay_ref, delay), (imped_ref, imped), (near_hist_ref, hist),
    ]
    started = copies(pairs, sems)
    lines_ref[...] = jnp.zeros(LINES_SHAPE, F32)
    wait(started[:4])
    here = at_ports(e_ref[2].reshape(NZ * NX, NY), own_ports(cell[...]))
    first = jnp.concatenate([node[...], cell[...]], 1).astype(F32)
    second = jnp.concatenate([cond[...], here[:, :HALF]], 1)
    sending = [payload(pay_out, pay_ref, sems.at[12], first, second)]
    wait(started[4:8])
    layers = [(ref, (c, z)) for ref in (e_ref, h_ref) for c in range(3) for z in range(NZ)]
    layers += [(ref, (z,)) for ref in (d_ref, g_ref) for z in range(NZ)]
    for k in range(0, LAYERS, 2):
        tiles = [ref[(*at, slice(NX - 8, NX))] for ref, at in layers[k : k + 2]]
        right_ref[k * DEEP : (k + 2) * DEEP] = jnp.concatenate([t[DEEP:] for t in tiles], 0)
        tiles = [ref[(*at, slice(0, 8))] for ref, at in layers[k : k + 2]]
        left_ref[k * DEEP : (k + 2) * DEEP] = jnp.concatenate([t[:DEEP] for t in tiles], 0)
    for k, (a, b) in enumerate(((right_ref, right_out), (left_ref, left_out))):
        sending.append(pltpu.make_async_copy(a, b, sems.at[13 + k]))
        sending[-1].start()
    wait(started[8:])
    lines_ref[0:1, 0:LANES] = far[...].astype(F32)
    lines_ref[1:2, 0:LANES] = delay[...].astype(F32)
    lines_ref[2:3, 0:LANES] = imped[...]
    for k in range(DEPTH):
        lines_ref[k : k + 1, LANES:] = hist[k]
    wait(sending)


def update_e(e_ref, h_ref, d_ref, g_ref, components, width):
    for z in range(NZ):
        hx, hy, hz = h_ref[0, z + 1], h_ref[1, z + 1], h_ref[2, z + 1]
        d, g = d_ref[z], g_ref[z]
        for c in components:
            if c == 0:
                own = hz[:width]
                curl = (own - last_y(own)) - (hy[:width] - h_ref[1, z, :width])
            elif c == 1:
                curl = (hx[:width] - h_ref[0, z, :width]) - (hz - last_x(hz))[:width]
            else:
                own = hx[:width]
                curl = (hy - last_x(hy))[:width] - (own - last_y(own))
            e_ref[c, z + 1, :width] = d * e_ref[c, z + 1, :width] + g * curl


def own_rows(ref):
    return ref.at[:, 1 : NZ + 1, 0:NX]


def k_start(
    e_in, h_in, d_in, g_in, right_ref, left_ref, cell_in, lines_ref, e_ref, h_ref, d_out, g_out, pre_ref, top_ref,
    d_ref, g_ref, cell_ref, sems,
):
    pairs = [
        (d_in, d_ref.at[:, 0:NX]), (g_in, g_ref.at[:, 0:NX]), (e_in, own_rows(e_ref)), (h_in, own_rows(h_ref)), (cell_in, cell_ref),
    ]
    started = copies(pairs, sems)
    for c in range(3):
        h_ref[c, 0] = jnp.zeros((GX, NY), F32)
        e_ref[c, 0] = jnp.zeros((GX, NY), F32)
        e_ref[c, NZ + 1] = jnp.zeros((GX, NY), F32)

    def tile(k):
        rows = slice(k * DEEP, (k + 1) * DEEP)
        return jnp.concatenate([left_ref[rows], right_ref[rows]], 0)

    for z in range(NZ):
        d_ref[z, NX:] = tile(6 * NZ + z)
        g_ref[z, NX:] = tile(7 * NZ + z)
    wait(started[:2])
    more = [pltpu.make_async_copy(d_ref, d_out, sems.at[5]), pltpu.make_async_copy(g_ref, g_out, sems.at[6])]
    for copy in more:
        copy.start()
    for c in range(3):
        for z in range(NZ):
            e_ref[c, z + 1, NX:] = tile(c * NZ + z)
            h_ref[c, z + 1, NX:] = tile(3 * NZ + c * NZ + z)
    wait(started[2:])
    update_e(e_ref, h_ref, d_ref, g_ref, (2,), GX)
    for c in range(2):
        top_ref[c * GX : (c + 1) * GX] = h_ref[c, NZ]
    ports = own_ports(cell_ref[...])
    pre = at_ports(e_ref[2, 1 : NZ + 1, :NX].reshape(NZ * NX, NY), ports)
    gain = at_ports(g_ref[:, :NX].reshape(NZ * NX, NY), ports)
    pre_ref[...] = jnp.broadcast_to(pre + pltpu.roll(gain, HALF, 1), (8, LANES))
    wait(more)


def low_onehots(node):
    return jnp.concatenate([ones_where(iota((LANES, LANES), 0) == node[t : t + 1] % LANES) for t in range(10)], 1)


def own_volts(w, lines, node, inverse_ref):
    high = node // LANES
    values = jnp.concatenate([w, lines], 0)
    spread = [jnp.where(iota((NB, LANES), 0) == high[t : t + 1], values[t : t + 1], 0.0) for t in range(10)]
    sources = dot3(jnp.concatenate(spread, 1), low_onehots(node), NT)
    total = jnp.zeros((LANES, LANES), F32)
    for t in range(NB):
        total = total + inverse_ref[0, :, t * LANES : (t + 1) * LANES] * sources[t : t + 1]
    return jnp.sum(total.T, 0, keepdims=True)


def node_values(volts, node):
    high = node // LANES
    picked = dot3(volts, low_onehots(node))
    rows = []
    for t in range(10):
        mine = jnp.where(iota((NB, LANES), 0) == high[t : t + 1], picked[:, t * LANES : (t + 1) * LANES], 0.0)
        rows.append(jnp.sum(mine, 0, keepdims=True))
    return jnp.concatenate(rows, 0)


def line_inputs(state_ref, n):
    own = n - state_ref[STATIC + 4 : STATIC + 5].astype(jnp.int32) + DEPTH
    below = n - state_ref[STATIC + 5 : STATIC + 6].astype(jnp.int32) + DEPTH
    return (
        hist_at(state_ref[FROM_ABOVE : FROM_ABOVE + 16], own),
        hist_at(state_ref[FROM_BELOW : FROM_BELOW + 16], below),
        hist_at(state_ref[OWN : OWN + 16], own),
    )


def next_volts(state_ref, inverse_ref, n):
    into_near, into_below, _ = line_inputs(state_ref, n)
    lines = -jnp.concatenate([into_near, into_below], 0)
    w = state_ref[COND : COND + 8] * state_ref[EZ : EZ + 8]
    return own_volts(w, lines, state_ref[NODE : NODE + 16].astype(jnp.int32), inverse_ref)


def payload(pay_out, pay_ref, sem, volts, pre):
    pay_ref[...] = jnp.broadcast_to(jnp.concatenate([volts, pre], 0)[None], PAY_SHAPE)
    copy = pltpu.make_async_copy(pay_ref, pay_out, sem)
    copy.start()
    return copy


def k_tables(
    got_ref, lines_ref, pre_ref, near_in, delay_in, imped_in, near_hist_in, far_hist_in, inverse_in,
    pay_out, state_ref,
    near_ref, delay_ref, imped_ref, near_hist_ref, far_hist_ref, inverse_ref, pay_ref, sems,
):
    pairs = [
        (near_in, near_ref), (delay_in, delay_ref), (imped_in, imped_ref),
        (near_hist_in, near_hist_ref), (far_hist_in, far_hist_ref), (inverse_in, inverse_ref),
    ]
    started = copies(pairs, sems)
    state_ref[...] = jnp.zeros((ROWS, LANES), F32)
    state_ref[NODE : NODE + 8] = lower(got_ref, 0)
    device = iota((8, LANES), 0) + 8 * (iota((8, LANES), 1) // HALF)
    state_ref[WHERE : WHERE + 8] = upper(got_ref, 0) + (device * (NZ * NX * NY)).astype(F32)
    state_ref[COND : COND + 8] = lower(got_ref, 1)
    state_ref[EZ : EZ + 8] = upper(got_ref, 1)
    far_below = lines_ref[0:1, 0:LANES]
    imped_below = jnp.where(row() == 0, 1.0, lines_ref[2:3, 0:LANES])
    wait(started[:5])
    near = near_ref[...].astype(F32)
    static = [near, far_below, imped_ref[...], imped_below, delay_ref[...].astype(F32), lines_ref[1:2, 0:LANES]]
    state_ref[NODE + 8 : NODE + 10] = jnp.concatenate(static[:2], 0)
    state_ref[STATIC : STATIC + 6] = jnp.concatenate(static, 0)
    for k in range(DEPTH):
        back = DEPTH - 1 - k
        state_ref[OWN + k : OWN + k + 1] = near_hist_ref[back]
        state_ref[FROM_ABOVE + k : FROM_ABOVE + k + 1] = far_hist_ref[back]
        state_ref[FROM_BELOW + k : FROM_BELOW + k + 1] = lines_ref[back : back + 1, LANES:]
    wait(started[5:])
    payload(pay_out, pay_ref, sems.at[6], next_volts(state_ref, inverse_ref, 0), pre_ref[0:1]).wait()


def block_row(k):
    block = column() + k
    return jnp.where(block < 0, block + 8, block % 8), block // 8, (block >= 0) & (block < NB)


def spread_currents(e_ref, where, drop):
    row_parts, at_y = [], []
    for k in (-1, 0, 1):
        packed, half, exists = block_row(k)
        pick = iota((8, LANES), 0) == packed
        cell = jnp.sum(jnp.where(pick, where, 0.0), 0, keepdims=True).astype(jnp.int32) % (NZ * NX * NY)
        values = jnp.sum(jnp.where(pick, drop, 0.0), 0, keepdims=True)
        x = (cell // NY) % NX + k * NX
        position = jnp.where((x >= 0) & (x < NX + DEEP), x, jnp.where((x < 0) & (x >= -DEEP), x + GX, -1))
        inside = (iota((1, LANES), 1) // HALF == half) & exists & (position >= 0)
        target = jnp.where(inside, (cell // (NX * NY)) * GX + position, -1)
        at_row = ones_where(iota((NZ * GX, LANES), 0) == target)
        row_parts.append(jnp.concatenate([at_row * part for part in split3(values)], 0))
        at_y.append(ones_where(iota((NY, LANES), 0) == cell % NY))
    spread = lax.dot_general(jnp.concatenate(row_parts, 1), jnp.concatenate(at_y, 1), NT, preferred_element_type=F32)
    rows = NZ * GX
    spread = spread[:rows] + (spread[rows : 2 * rows] + spread[2 * rows :])
    for z in range(NZ):
        e_ref[2, z + 1] = e_ref[2, z + 1] - spread[z * GX : (z + 1) * GX]


def k_currents(n, last, got_ref, e_in, state_in, e_ref, state_ref, *sends):
    pre = lower(got_ref, 1)
    if n == 0:
        state_ref[GAIN : GAIN + 8] = upper(got_ref, 1)
    at_nodes = node_values(got_ref[:, 0, :], state_ref[NODE : NODE + 16].astype(jnp.int32))
    where = state_ref[WHERE : WHERE + 8]
    current = state_ref[COND : COND + 8] * (state_ref[EZ : EZ + 8] - at_nodes[0:8])
    shared = current
    for k in range(1, LANES):
        same = pltpu.roll(where, k, 1) == where
        shared = shared + jnp.where(same, pltpu.roll(current, k, 1), 0.0)
    gain = state_ref[GAIN : GAIN + 8]
    state_ref[EZ : EZ + 8] = pre - gain * shared

    into_near, into_below, into_own = line_inputs(state_ref, n)
    out_near = -2.0 * at_nodes[8:9] / state_ref[STATIC + 2 : STATIC + 3] - into_near
    out_below = -2.0 * at_nodes[9:10] / state_ref[STATIC + 3 : STATIC + 4] - into_below
    top = jnp.where(row() == NF - 1, -into_own, 0.0)
    state_ref[WAVE : WAVE + 2] = jnp.concatenate([out_near, top], 0)

    spread_currents(e_ref, where, gain * current)

    down_ref = sends[-1]
    for c in range(2):
        down_ref[c * GX : (c + 1) * GX] = e_ref[c, 1]
    down_ref[2 * GX :] = jnp.zeros((8, NY), F32)
    down_ref[2 * GX : 2 * GX + 1, 0:LANES] = out_below
    if not last:
        up_ref = sends[0]
        for c in range(3):
            up_ref[c * GX : (c + 1) * GX] = e_ref[c, NZ]
        up_ref[3 * GX :] = jnp.zeros((8, NY), F32)
        up_ref[3 * GX : 3 * GX + 1, 0:LANES] = out_near


def new_h(e_ref, h_ref, layer, ex_above, ey_above):
    scale = jnp.where((iota((GX, 1), 0) >= GX - DEEP) & (column() == 0), 0.0, 0.5)
    ex, ey, ez = e_ref[0, layer], e_ref[1, layer], e_ref[2, layer]
    if layer == 0:
        scale = jnp.where(row() == 0, 0.0, scale)
    hx = h_ref[0, layer] - scale * ((next_y(ez) - ez) - (ey_above - ey))
    hy = h_ref[1, layer] - scale * ((ex_above - ex) - (next_x(ez) - ez))
    hz = h_ref[2, layer] - scale * ((next_x(ey) - ey) - (next_y(ex) - ex))
    return hx, hy, hz


def update_h(e_ref, h_ref, layer):
    for c, value in enumerate(new_h(e_ref, h_ref, layer, e_ref[0, layer + 1], e_ref[1, layer + 1])):
        h_ref[c, layer] = value


def k_inner_h(e_ref, h_in, h_ref):
    for layer in range(1, NZ):
        update_h(e_ref, h_ref, layer)


def k_inner_last(e_ref, h_in, h_ref, e_out, h_out, sems):
    first = copies([(own_rows(e_ref), e_out)], sems)
    for layer in range(1, NZ):
        update_h(e_ref, h_ref, layer)
    second = pltpu.make_async_copy(h_ref.at[:, 1:NZ, 0:NX], h_out.at[:, 0 : NZ - 1], sems.at[1])
    second.start()
    wait(first)
    second.wait()


def k_volts(
    n, last, up_ref, down_ref, d_ref, g_ref, inverse_ref, cell_ref, e_in, h_in, state_in,
    e_ref, h_ref, state_ref, pay_out, *rest,
):
    pay_ref, sem = rest[-2:]
    at = n - 1 + DEPTH
    state_ref[OWN + at : OWN + at + 1] = state_ref[WAVE : WAVE + 1]
    state_ref[FROM_ABOVE + at : FROM_ABOVE + at + 1] = down_ref[2 * GX : 2 * GX + 1, 0:LANES] + state_ref[WAVE + 1 : WAVE + 2]
    state_ref[FROM_BELOW + at : FROM_BELOW + at + 1] = up_ref[3 * GX : 3 * GX + 1, 0:LANES]
    volts = next_volts(state_ref, inverse_ref, n)
    if last:
        rest[0][...] = volts
    for c in range(3):
        e_ref[c, 0] = up_ref[c * GX : (c + 1) * GX]
    for c in range(2):
        e_ref[c, NZ + 1] = down_ref[c * GX : (c + 1) * GX]
    update_h(e_ref, h_ref, 0)
    update_h(e_ref, h_ref, NZ)
    update_e(e_ref, h_ref, d_ref, g_ref, (2,), GX)
    pre = at_ports(e_ref[2, 1 : NZ + 1, :NX].reshape(NZ * NX, NY), own_ports(cell_ref[...]))
    payload(pay_out, pay_ref, sem, volts, pre).wait()


def k_exy_first(top_ref, d_ref, g_ref, e_in, h_in, e_ref, h_ref):
    for c in range(2):
        h_ref[c, 0] = top_ref[c * GX : (c + 1) * GX]
    update_e(e_ref, h_ref, d_ref, g_ref, (0, 1), GX)


def k_exy(h_ref, d_ref, g_ref, e_in, e_ref):
    update_e(e_ref, h_ref, d_ref, g_ref, (0, 1), GX)


def k_last(down_ref, state_ref, e_ref, h_ref, h_in, h_out, wave_out, layer_ref, sem):
    for c, value in enumerate(new_h(e_ref, h_ref, NZ, down_ref[0:GX], down_ref[GX : 2 * GX])):
        layer_ref[c] = value[:NX]
    copy = pltpu.make_async_copy(layer_ref, h_out.at[:, NZ - 1], sem)
    copy.start()
    above = down_ref[2 * GX : 2 * GX + 1, 0:LANES] + state_ref[WAVE + 1 : WAVE + 2]
    wave_out[...] = jnp.concatenate([state_ref[WAVE : WAVE + 1], above], 0)[None]
    copy.wait()


def local(
    e_field,
    h_field,
    e_decay,
    e_gain,
    port_cell,
    port_node,
    port_conductance,
    inverse,
    line_near,
    line_far,
    line_delay,
    line_imped,
    hist_near,
    hist_far,
):
    hist_near = jnp.transpose(hist_near, (1, 0, 2))
    hist_far = jnp.transpose(hist_far, (1, 0, 2))
    hist_shape = pltpu.VMEM((DEPTH, 1, LANES), F32)
    line = pltpu.VMEM((1, LANES), F32)
    line_int = pltpu.VMEM((1, LANES), jnp.int32)
    ports_int = pltpu.VMEM((1, HALF), jnp.int32)
    block = pltpu.VMEM((NZ, NX, NY), F32)
    pay_scratch = pltpu.VMEM(PAY_SHAPE, F32)
    side = pltpu.VMEM(SIDE_SHAPE, F32)
    wide = pltpu.VMEM(WIDE, F32)

    pay, lines, to_right, to_left = call(
        k_first,
        [PAY_SHAPE, LINES_SHAPE, SIDE_SHAPE, SIDE_SHAPE],
        e_field, h_field, e_decay, e_gain, port_cell, port_node, port_conductance, line_far, line_delay, line_imped, hist_near,
        far=range(11),
        far_out=(0, 2, 3),
        scratch=[
            pltpu.VMEM(FIELD, F32), pltpu.VMEM(FIELD, F32), block, block, ports_int, ports_int, pltpu.VMEM((1, HALF), F32),
            line_int, line_int, line, hist_shape, pay_scratch, side, side, pltpu.SemaphoreType.DMA((15,)),
        ],
        name="first",
    )
    got = exchanged(pay)
    lines = shifted(lines, "fz", 1)
    e, h, d, g, pre, top = call(
        k_start,
        [E_SHAPE, H_SHAPE, WIDE, WIDE, (8, LANES), TOP_SHAPE],
        e_field, h_field, e_decay, e_gain, shifted(to_right, "fxy", 1), shifted(to_left, "fxy", -1), port_cell, lines,
        far=(0, 1, 2, 3, 6),
        far_out=(2, 3),
        scratch=[wide, wide, ports_int, pltpu.SemaphoreType.DMA((7,))],
        name="start",
    )
    pay, state = call(
        k_tables,
        [PAY_SHAPE, (ROWS, LANES)],
        got, lines, pre, line_near, line_delay, line_imped, hist_near, hist_far, inverse,
        far=range(3, 9),
        scratch=[
            line_int, line_int, line, hist_shape, hist_shape,
            pltpu.VMEM((1, LANES, NB * LANES), F32), pay_scratch, pltpu.SemaphoreType.DMA((7,)),
        ],
        far_out=(0,),
        name="tables",
    )
    for n in range(STEPS):
        last = n == STEPS - 1
        got = exchanged(pay)
        if n == 0:
            e, h = call(
                k_exy_first,
                [E_SHAPE, H_SHAPE],
                shifted(top, "fz", 1), d, g, e, h,
                alias={3: 0, 4: 1},
                name="exy_first",
            )
        else:
            (e,) = call(k_exy, [E_SHAPE], h, d, g, e, alias={3: 0}, name="exy")
        e, state, *sends = call(
            functools.partial(k_currents, n, last),
            [E_SHAPE, (ROWS, LANES)] + ([] if last else [UP_SHAPE]) + [DOWN_SHAPE],
            got, e, state,
            alias={1: 0, 2: 1},
            name="currents",
        )
        down = shifted(sends[-1], "fz", -1)
        if last:
            break
        up = shifted(sends[0], "fz", 1)
        (h,) = call(k_inner_h, [H_SHAPE], e, h, alias={1: 0}, name="inner_h")
        e, h, state, pay, *node_volt = call(
            functools.partial(k_volts, n + 1, n + 1 == STEPS - 1),
            [E_SHAPE, H_SHAPE, (ROWS, LANES), PAY_SHAPE] + ([(1, LANES)] if n + 1 == STEPS - 1 else []),
            up, down, d, g, inverse, port_cell, e, h, state,
            alias={6: 0, 7: 1, 8: 2},
            far_out=(3,),
            scratch=[pay_scratch, pltpu.SemaphoreType.DMA],
            name="volts",
        )
    h, e_out, h_out = call(
        k_inner_last,
        [H_SHAPE, FIELD, FIELD],
        e, h,
        alias={1: 0},
        far_out=(1, 2),
        scratch=[pltpu.SemaphoreType.DMA((2,))],
        name="inner_last",
    )
    h_out, line_wave = call(
        k_last,
        [FIELD, (1, 2, LANES)],
        down, state, e, h, h_out,
        alias={4: 0},
        far=(4,),
        far_out=(0,),
        scratch=[pltpu.VMEM((3, NX, NY), F32), pltpu.SemaphoreType.DMA],
        name="last",
    )
    return e_out, h_out, node_volt[0], line_wave


def solution(mesh):
    placed = (
        P(None, "fz", "fxy", None),
        P(None, "fz", "fxy", None),
        P("fz", "fxy", None),
        P("fz", "fxy", None),
        P("fz", "fxy"),
        P("fz", "fxy"),
        P("fz", "fxy"),
        P("fz", "fxy", None),
        P("fz", None),
        P("fz", None),
        P("fz", None),
        P("fz", None),
        P("fz", None, None),
        P("fz", None, None),
    )
    return jax.shard_map(
        local,
        mesh=mesh,
        in_specs=placed,
        out_specs=(
            P(None, "fz", "fxy", None),
            P(None, "fz", "fxy", None),
            P("fz", "fxy"),
            P("fz", None, None),
        ),
        check_vma=False,
    )
```

```python
import functools

import jax
import jax.numpy as jnp
from jax import lax
from jax.experimental import pallas as pl
from jax.experimental.pallas import tpu as pltpu
from jax.sharding import PartitionSpec as P

STEPS = 4
F32 = jnp.float32
BF16 = jnp.bfloat16
NZ = 8
NX = 16
NY = 512
GX = 24
DEEP = 4
NF = 32
NB = 16
HALF = 64
LANES = 128
DEPTH = 6
VMEM = pl.BlockSpec(memory_space=pltpu.VMEM)
ANY = pl.BlockSpec(memory_space=pltpu.HBM)
NT = (((1,), (1,)), ((), ()))
NODE, WHERE, COND, GAIN, EZ, STATIC, OWN, FROM_ABOVE, FROM_BELOW, WAVE, ROWS = 0, 16, 24, 32, 40, 48, 56, 72, 88, 104, 112
E_SHAPE = (3, NZ + 2, GX, NY)
H_SHAPE = (3, NZ + 1, GX, NY)
PAY_SHAPE = (NB, 2, LANES)
LAYERS = 8 * NZ
SIDE_SHAPE = (LAYERS * DEEP, NY)
WIDE = (NZ, GX, NY)
UP_SHAPE, DOWN_SHAPE = (3 * GX + 8, NY), (2 * GX + 8, NY)
BELOW_SHAPE, CORNER_SHAPE = (2 * NX + 8, NY), (2 * DEEP, NY)
FIELD = (3, NZ, NX, NY)


def call(kernel, outs, *args, alias=None, name=None, far=(), far_out=(), scratch=(), room=40 << 20):
    args = [pltpu.with_memory_space_constraint(x, pltpu.HBM) if k in far else x for k, x in enumerate(args)]
    return pl.pallas_call(
        kernel,
        out_shape=[pltpu.HBM(s, F32) if k in far_out else jax.ShapeDtypeStruct(s, F32) for k, s in enumerate(outs)],
        in_specs=[ANY if k in far else VMEM for k in range(len(args))],
        out_specs=[ANY if k in far_out else VMEM for k in range(len(outs))],
        scratch_shapes=list(scratch),
        input_output_aliases=alias or {},
        name=name,
        compiler_params=pltpu.CompilerParams(vmem_limit_bytes=room),
    )(*args)


def shifted(value, axis, by):
    devices = lax.axis_size(axis)
    pairs = [(i, i + by) for i in range(devices) if 0 <= i + by < devices]
    return lax.ppermute(value, axis, pairs)


def shifted_up(value, by):
    pairs = [(s * NB + j, (s + 1) * NB + j + by) for s in range(NF - 1) for j in range(NB) if 0 <= j + by < NB]
    return lax.ppermute(value, ("fz", "fxy"), pairs)


def exchanged(value):
    return lax.all_to_all(value, "fxy", 0, 0, tiled=True)


def iota(shape, dim):
    return lax.broadcasted_iota(jnp.int32, shape, dim)


def column():
    return lax.axis_index("fxy")


def row():
    return lax.axis_index("fz")


def split3(value):
    high = value.astype(BF16)
    rest = value - high.astype(F32)
    middle = rest.astype(BF16)
    low = (rest - middle.astype(F32)).astype(BF16)
    return high, middle, low


def dot3(value, onehot, dims=(((1,), (0,)), ((), ()))):
    rows = value.shape[0]
    parts = jnp.concatenate(split3(value), 0)
    product = lax.dot_general(parts, onehot, dims, preferred_element_type=F32)
    return product[:rows] + (product[rows : 2 * rows] + product[2 * rows :])


def ones_where(condition):
    return jnp.where(condition, 1.0, 0.0).astype(BF16)


def next_y(f):
    rolled = pltpu.roll(f, NY - 1, 1)
    return jnp.where(iota(f.shape, 1) == NY - 1, 0.0, rolled)


def last_y(f):
    rolled = pltpu.roll(f, 1, 1)
    return jnp.where(iota(f.shape, 1) == 0, 0.0, rolled)


def next_x(f):
    return jnp.concatenate([f[1:], f[:1]], 0)


def last_x(f):
    return jnp.concatenate([f[GX - 1 :], f[: GX - 1]], 0)


def copies(pairs, sems):
    started = [pltpu.make_async_copy(a, b, sems.at[k]) for k, (a, b) in enumerate(pairs)]
    for copy in started:
        copy.start()
    return started


def wait(started):
    for copy in started:
        copy.wait()


def lower(got_ref, f):
    lane = iota((8, LANES), 1)
    return jnp.where(lane < HALF, got_ref[0:8, f, :], pltpu.roll(got_ref[8:16, f, :], HALF, 1))


def upper(got_ref, f):
    lane = iota((8, LANES), 1)
    return jnp.where(lane < HALF, pltpu.roll(got_ref[0:8, f, :], HALF, 1), got_ref[8:16, f, :])


def own_ports(cell):
    cell = jnp.concatenate([cell, cell], 1)
    mine = iota((1, LANES), 1) < HALF
    at_row = ones_where((iota((NZ * NX, LANES), 0) == cell // NY) & mine)
    at_y = ones_where(iota((NY, LANES), 0) == cell % NY)
    return at_row, at_y


def at_ports(field, ports):
    at_row, at_y = ports
    return jnp.sum(dot3(field, at_y) * at_row.astype(F32), 0, keepdims=True)


def hist_at(hist, position):
    out = jnp.zeros((1, LANES), F32)
    for k in range(DEPTH + STEPS):
        out = jnp.where(position == k, hist[k : k + 1], out)
    return out


def k_first(
    e_in, h_in, d_in, g_in, cell_ref, node_ref, cond_ref, far_ref, delay_ref, imped_ref, near_hist_ref,
    pay_out, below_ref, corner_right, corner_left, right_out, left_out,
    e_ref, h_ref, d_ref, g_ref, cell, node, cond, far, delay, imped, hist, pay_ref, right_ref, left_ref, sems,
):
    pairs = [
        (cell_ref, cell), (node_ref, node), (cond_ref, cond), (e_in.at[2], e_ref.at[2]),
        (e_in.at[0:2], e_ref.at[0:2]), (h_in, h_ref), (d_in, d_ref), (g_in, g_ref),
        (far_ref, far), (delay_ref, delay), (imped_ref, imped), (near_hist_ref, hist),
    ]
    started = copies(pairs, sems)
    below_ref[2 * NX :] = jnp.zeros((8, NY), F32)
    wait(started[:4])
    here = at_ports(e_ref[2].reshape(NZ * NX, NY), own_ports(cell[...]))
    first = jnp.concatenate([node[...], cell[...]], 1).astype(F32)
    second = jnp.concatenate([cond[...], here[:, :HALF]], 1)
    sending = [payload(pay_out, pay_ref, sems.at[12], first, second)]
    wait(started[4:8])
    layers = [(ref, (c, z)) for ref in (e_ref, h_ref) for c in range(3) for z in range(NZ)]
    layers += [(ref, (z,)) for ref in (d_ref, g_ref) for z in range(NZ)]
    for k in range(0, LAYERS, 2):
        tiles = [ref[(*at, slice(NX - 8, NX))] for ref, at in layers[k : k + 2]]
        right_ref[k * DEEP : (k + 2) * DEEP] = jnp.concatenate([t[DEEP:] for t in tiles], 0)
        tiles = [ref[(*at, slice(0, 8))] for ref, at in layers[k : k + 2]]
        left_ref[k * DEEP : (k + 2) * DEEP] = jnp.concatenate([t[:DEEP] for t in tiles], 0)
    for k, (a, b) in enumerate(((right_ref, right_out), (left_ref, left_out))):
        sending.append(pltpu.make_async_copy(a, b, sems.at[13 + k]))
        sending[-1].start()
    for c in range(2):
        below_ref[c * NX : (c + 1) * NX] = h_ref[c, NZ - 1]
        corner_right[c * DEEP : (c + 1) * DEEP] = h_ref[c, NZ - 1, NX - DEEP :]
        corner_left[c * DEEP : (c + 1) * DEEP] = h_ref[c, NZ - 1, :DEEP]
    wait(started[8:])
    below_ref[2 * NX : 2 * NX + 1, 0:LANES] = far[...].astype(F32)
    below_ref[2 * NX + 1 : 2 * NX + 2, 0:LANES] = delay[...].astype(F32)
    below_ref[2 * NX + 2 : 2 * NX + 3, 0:LANES] = imped[...]
    for k in range(DEPTH):
        below_ref[2 * NX + k : 2 * NX + k + 1, LANES : 2 * LANES] = hist[k]
    wait(sending)


def update_e(e_ref, h_ref, d_ref, g_ref, components, width):
    for z in range(NZ):
        hx, hy, hz = h_ref[0, z + 1], h_ref[1, z + 1], h_ref[2, z + 1]
        d, g = d_ref[z], g_ref[z]
        for c in components:
            if c == 0:
                own = hz[:width]
                curl = (own - last_y(own)) - (hy[:width] - h_ref[1, z, :width])
            elif c == 1:
                curl = (hx[:width] - h_ref[0, z, :width]) - (hz - last_x(hz))[:width]
            else:
                own = hx[:width]
                curl = (hy - last_x(hy))[:width] - (own - last_y(own))
            e_ref[c, z + 1, :width] = d * e_ref[c, z + 1, :width] + g * curl


def own_rows(ref):
    return ref.at[:, 1 : NZ + 1, 0:NX]


def k_start(
    e_in, h_in, d_in, g_in, cell_in, near_in, delay_in, imped_in, near_hist_in, far_hist_in,
    right_in, left_in, below_ref, corner_right, corner_left,
    e_ref, h_ref, d_out, g_out, pre_ref, state_ref,
    right_ref, left_ref, d_ref, g_ref, cell_ref, near_ref, delay_ref, imped_ref, near_hist_ref, far_hist_ref, sems,
):
    pairs = [
        (d_in, d_ref.at[:, 0:NX]), (g_in, g_ref.at[:, 0:NX]), (e_in, own_rows(e_ref)), (h_in, own_rows(h_ref)), (cell_in, cell_ref),
        (near_in, near_ref), (delay_in, delay_ref), (imped_in, imped_ref), (near_hist_in, near_hist_ref), (far_hist_in, far_hist_ref),
    ]
    sides = copies([(right_in, right_ref), (left_in, left_ref)], sems.at[12:14])
    started = copies(pairs, sems)
    for c in range(3):
        h_ref[c, 0] = jnp.zeros((GX, NY), F32)
        e_ref[c, 0] = jnp.zeros((GX, NY), F32)
        e_ref[c, NZ + 1] = jnp.zeros((GX, NY), F32)
    wait(sides)

    def tile(k):
        rows = slice(k * DEEP, (k + 1) * DEEP)
        return jnp.concatenate([left_ref[rows], right_ref[rows]], 0)

    for z in range(NZ):
        d_ref[z, NX:] = tile(6 * NZ + z)
        g_ref[z, NX:] = tile(7 * NZ + z)
    wait(started[:2])
    more = [pltpu.make_async_copy(d_ref, d_out, sems.at[10]), pltpu.make_async_copy(g_ref, g_out, sems.at[11])]
    for copy in more:
        copy.start()
    for c in range(3):
        for z in range(NZ):
            e_ref[c, z + 1, NX:] = tile(c * NZ + z)
            h_ref[c, z + 1, NX:] = tile(3 * NZ + c * NZ + z)
    wait(started[2:])
    update_e(e_ref, h_ref, d_ref, g_ref, (2,), GX)
    for c in range(2):
        rows = slice(c * DEEP, (c + 1) * DEEP)
        h_ref[c, 0, :NX] = below_ref[c * NX : (c + 1) * NX]
        h_ref[c, 0, NX:] = jnp.concatenate([corner_left[rows], corner_right[rows]], 0)
    ports = own_ports(cell_ref[...])
    pre = at_ports(e_ref[2, 1 : NZ + 1, :NX].reshape(NZ * NX, NY), ports)
    gain = at_ports(g_ref[:, :NX].reshape(NZ * NX, NY), ports)
    pre_ref[...] = jnp.broadcast_to(pre + pltpu.roll(gain, HALF, 1), (8, LANES))

    state_ref[...] = jnp.zeros((ROWS, LANES), F32)
    far_below = below_ref[2 * NX : 2 * NX + 1, 0:LANES]
    imped_below = jnp.where(row() == 0, 1.0, below_ref[2 * NX + 2 : 2 * NX + 3, 0:LANES])
    delay_below = below_ref[2 * NX + 1 : 2 * NX + 2, 0:LANES]
    near = near_ref[...].astype(F32)
    static = [near, far_below, imped_ref[...], imped_below, delay_ref[...].astype(F32), delay_below]
    state_ref[NODE + 8 : NODE + 10] = jnp.concatenate(static[:2], 0)
    state_ref[STATIC : STATIC + 6] = jnp.concatenate(static, 0)
    for k in range(DEPTH):
        back = DEPTH - 1 - k
        state_ref[OWN + k : OWN + k + 1] = near_hist_ref[back]
        state_ref[FROM_ABOVE + k : FROM_ABOVE + k + 1] = far_hist_ref[back]
        state_ref[FROM_BELOW + k : FROM_BELOW + k + 1] = below_ref[2 * NX + back : 2 * NX + back + 1, LANES : 2 * LANES]
    wait(more)


def low_onehots(node):
    return jnp.concatenate([ones_where(iota((LANES, LANES), 0) == node[t : t + 1] % LANES) for t in range(10)], 1)


def own_volts(w, lines, node, inverse_ref, ready):
    high = node // LANES
    values = jnp.concatenate([w, lines], 0)
    spread = [jnp.where(iota((NB, LANES), 0) == high[t : t + 1], values[t : t + 1], 0.0) for t in range(10)]
    sources = dot3(jnp.concatenate(spread, 1), low_onehots(node), NT)
    ready()
    total = jnp.zeros((LANES, LANES), F32)
    for t in range(NB):
        total = total + inverse_ref[0, :, t * LANES : (t + 1) * LANES] * sources[t : t + 1]
    return jnp.sum(total.T, 0, keepdims=True)


def node_values(volts, node):
    high = node // LANES
    picked = dot3(volts, low_onehots(node))
    rows = []
    for t in range(10):
        mine = jnp.where(iota((NB, LANES), 0) == high[t : t + 1], picked[:, t * LANES : (t + 1) * LANES], 0.0)
        rows.append(jnp.sum(mine, 0, keepdims=True))
    return jnp.concatenate(rows, 0)


def line_inputs(state_ref, n):
    own = n - state_ref[STATIC + 4 : STATIC + 5].astype(jnp.int32) + DEPTH
    below = n - state_ref[STATIC + 5 : STATIC + 6].astype(jnp.int32) + DEPTH
    return (
        hist_at(state_ref[FROM_ABOVE : FROM_ABOVE + 16], own),
        hist_at(state_ref[FROM_BELOW : FROM_BELOW + 16], below),
        hist_at(state_ref[OWN : OWN + 16], own),
    )


def next_volts(state_ref, inverse_ref, n, ready=lambda: None):
    into_near, into_below, _ = line_inputs(state_ref, n)
    lines = -jnp.concatenate([into_near, into_below], 0)
    w = state_ref[COND : COND + 8] * state_ref[EZ : EZ + 8]
    return own_volts(w, lines, state_ref[NODE : NODE + 16].astype(jnp.int32), inverse_ref, ready)


def payload(pay_out, pay_ref, sem, volts, pre):
    pay_ref[...] = jnp.broadcast_to(jnp.concatenate([volts, pre], 0)[None], PAY_SHAPE)
    copy = pltpu.make_async_copy(pay_ref, pay_out, sem)
    copy.start()
    return copy


def k_tables(got_ref, pre_ref, inverse_in, state_in, pay_out, state_ref, inverse_ref, pay_ref, sems):
    started = copies([(inverse_in, inverse_ref)], sems)
    state_ref[NODE : NODE + 8] = lower(got_ref, 0)
    device = iota((8, LANES), 0) + 8 * (iota((8, LANES), 1) // HALF)
    state_ref[WHERE : WHERE + 8] = upper(got_ref, 0) + (device * (NZ * NX * NY)).astype(F32)
    state_ref[COND : COND + 8] = lower(got_ref, 1)
    state_ref[EZ : EZ + 8] = upper(got_ref, 1)
    volts = next_volts(state_ref, inverse_ref, 0, lambda: wait(started))
    payload(pay_out, pay_ref, sems.at[1], volts, pre_ref[0:1]).wait()


def block_row(k):
    block = column() + k
    return jnp.where(block < 0, block + 8, block % 8), block // 8, (block >= 0) & (block < NB)


def spread_currents(e_ref, where, drop):
    row_parts, at_y = [], []
    for k in (-1, 0, 1):
        packed, half, exists = block_row(k)
        pick = iota((8, LANES), 0) == packed
        cell = jnp.sum(jnp.where(pick, where, 0.0), 0, keepdims=True).astype(jnp.int32) % (NZ * NX * NY)
        values = jnp.sum(jnp.where(pick, drop, 0.0), 0, keepdims=True)
        x = (cell // NY) % NX + k * NX
        position = jnp.where((x >= 0) & (x < NX + DEEP), x, jnp.where((x < 0) & (x >= -DEEP), x + GX, -1))
        inside = (iota((1, LANES), 1) // HALF == half) & exists & (position >= 0)
        target = jnp.where(inside, (cell // (NX * NY)) * GX + position, -1)
        at_row = ones_where(iota((NZ * GX, LANES), 0) == target)
        row_parts.append(jnp.concatenate([at_row * part for part in split3(values)], 0))
        at_y.append(ones_where(iota((NY, LANES), 0) == cell % NY))
    spread = lax.dot_general(jnp.concatenate(row_parts, 1), jnp.concatenate(at_y, 1), NT, preferred_element_type=F32)
    rows = NZ * GX
    spread = spread[:rows] + (spread[rows : 2 * rows] + spread[2 * rows :])
    for z in range(NZ):
        e_ref[2, z + 1] = e_ref[2, z + 1] - spread[z * GX : (z + 1) * GX]


def k_currents(n, last, got_ref, e_in, state_in, e_ref, state_ref, *sends):
    pre = lower(got_ref, 1)
    if n == 0:
        state_ref[GAIN : GAIN + 8] = upper(got_ref, 1)
    at_nodes = node_values(got_ref[:, 0, :], state_ref[NODE : NODE + 16].astype(jnp.int32))
    where = state_ref[WHERE : WHERE + 8]
    current = state_ref[COND : COND + 8] * (state_ref[EZ : EZ + 8] - at_nodes[0:8])
    shared = current
    for k in range(1, LANES):
        same = pltpu.roll(where, k, 1) == where
        shared = shared + jnp.where(same, pltpu.roll(current, k, 1), 0.0)
    gain = state_ref[GAIN : GAIN + 8]
    state_ref[EZ : EZ + 8] = pre - gain * shared

    into_near, into_below, into_own = line_inputs(state_ref, n)
    out_near = -2.0 * at_nodes[8:9] / state_ref[STATIC + 2 : STATIC + 3] - into_near
    out_below = -2.0 * at_nodes[9:10] / state_ref[STATIC + 3 : STATIC + 4] - into_below
    top = jnp.where(row() == NF - 1, -into_own, 0.0)
    state_ref[WAVE : WAVE + 2] = jnp.concatenate([out_near, top], 0)

    spread_currents(e_ref, where, gain * current)

    down_ref = sends[-1]
    for c in range(2):
        down_ref[c * GX : (c + 1) * GX] = e_ref[c, 1]
    down_ref[2 * GX :] = jnp.zeros((8, NY), F32)
    down_ref[2 * GX : 2 * GX + 1, 0:LANES] = out_below
    if not last:
        up_ref = sends[0]
        for c in range(3):
            up_ref[c * GX : (c + 1) * GX] = e_ref[c, NZ]
        up_ref[3 * GX :] = jnp.zeros((8, NY), F32)
        up_ref[3 * GX : 3 * GX + 1, 0:LANES] = out_near


def new_h(e_ref, h_ref, layer, ex_above, ey_above):
    scale = jnp.where((iota((GX, 1), 0) >= GX - DEEP) & (column() == 0), 0.0, 0.5)
    ex, ey, ez = e_ref[0, layer], e_ref[1, layer], e_ref[2, layer]
    if layer == 0:
        scale = jnp.where(row() == 0, 0.0, scale)
    hx = h_ref[0, layer] - scale * ((next_y(ez) - ez) - (ey_above - ey))
    hy = h_ref[1, layer] - scale * ((ex_above - ex) - (next_x(ez) - ez))
    hz = h_ref[2, layer] - scale * ((next_x(ey) - ey) - (next_y(ex) - ex))
    return hx, hy, hz


def update_h(e_ref, h_ref, layer):
    for c, value in enumerate(new_h(e_ref, h_ref, layer, e_ref[0, layer + 1], e_ref[1, layer + 1])):
        h_ref[c, layer] = value


def k_inner_h(e_ref, h_in, h_ref):
    for layer in range(1, NZ):
        update_h(e_ref, h_ref, layer)


def k_inner_last(e_ref, h_in, h_ref, e_out, h_out, sems):
    first = copies([(own_rows(e_ref), e_out)], sems)
    for layer in range(1, NZ):
        update_h(e_ref, h_ref, layer)
    second = pltpu.make_async_copy(h_ref.at[:, 1:NZ, 0:NX], h_out.at[:, 0 : NZ - 1], sems.at[1])
    second.start()
    wait(first)
    second.wait()


def k_volts(
    n, last, up_ref, down_ref, d_ref, g_ref, inverse_ref, cell_ref, e_in, h_in, state_in,
    e_ref, h_ref, state_ref, pay_out, *rest,
):
    pay_ref, sem = rest[-2:]
    at = n - 1 + DEPTH
    state_ref[OWN + at : OWN + at + 1] = state_ref[WAVE : WAVE + 1]
    state_ref[FROM_ABOVE + at : FROM_ABOVE + at + 1] = down_ref[2 * GX : 2 * GX + 1, 0:LANES] + state_ref[WAVE + 1 : WAVE + 2]
    state_ref[FROM_BELOW + at : FROM_BELOW + at + 1] = up_ref[3 * GX : 3 * GX + 1, 0:LANES]
    volts = next_volts(state_ref, inverse_ref, n)
    if last:
        rest[1][...] = volts
        sending = pltpu.make_async_copy(rest[1], rest[0], rest[2])
        sending.start()
    for c in range(3):
        e_ref[c, 0] = up_ref[c * GX : (c + 1) * GX]
    for c in range(2):
        e_ref[c, NZ + 1] = down_ref[c * GX : (c + 1) * GX]
    update_h(e_ref, h_ref, 0)
    update_h(e_ref, h_ref, NZ)
    update_e(e_ref, h_ref, d_ref, g_ref, (2,), GX)
    pre = at_ports(e_ref[2, 1 : NZ + 1, :NX].reshape(NZ * NX, NY), own_ports(cell_ref[...]))
    payload(pay_out, pay_ref, sem, volts, pre).wait()
    if last:
        sending.wait()


def k_exy(h_ref, d_ref, g_ref, e_in, e_ref):
    update_e(e_ref, h_ref, d_ref, g_ref, (0, 1), GX)


def k_last(down_ref, state_ref, e_ref, h_ref, h_in, h_out, wave_out, layer_ref, wave_ref, sems):
    above = down_ref[2 * GX : 2 * GX + 1, 0:LANES] + state_ref[WAVE + 1 : WAVE + 2]
    wave_ref[...] = jnp.concatenate([state_ref[WAVE : WAVE + 1], above], 0)[None]
    sending = copies([(wave_ref, wave_out)], sems)
    for c, value in enumerate(new_h(e_ref, h_ref, NZ, down_ref[0:GX], down_ref[GX : 2 * GX])):
        layer_ref[c] = value[:NX]
    sending.append(pltpu.make_async_copy(layer_ref, h_out.at[:, NZ - 1], sems.at[1]))
    sending[1].start()
    wait(sending)


def local(
    e_field,
    h_field,
    e_decay,
    e_gain,
    port_cell,
    port_node,
    port_conductance,
    inverse,
    line_near,
    line_far,
    line_delay,
    line_imped,
    hist_near,
    hist_far,
):
    hist_near = jnp.transpose(hist_near, (1, 0, 2))
    hist_far = jnp.transpose(hist_far, (1, 0, 2))
    hist_shape = pltpu.VMEM((DEPTH, 1, LANES), F32)
    line = pltpu.VMEM((1, LANES), F32)
    line_int = pltpu.VMEM((1, LANES), jnp.int32)
    ports_int = pltpu.VMEM((1, HALF), jnp.int32)
    block = pltpu.VMEM((NZ, NX, NY), F32)
    pay_scratch = pltpu.VMEM(PAY_SHAPE, F32)
    side = pltpu.VMEM(SIDE_SHAPE, F32)
    wide = pltpu.VMEM(WIDE, F32)

    pay, below, corner_right, corner_left, to_right, to_left = call(
        k_first,
        [PAY_SHAPE, BELOW_SHAPE, CORNER_SHAPE, CORNER_SHAPE, SIDE_SHAPE, SIDE_SHAPE],
        e_field, h_field, e_decay, e_gain, port_cell, port_node, port_conductance, line_far, line_delay, line_imped, hist_near,
        far=range(11),
        far_out=(0, 4, 5),
        scratch=[
            pltpu.VMEM(FIELD, F32), pltpu.VMEM(FIELD, F32), block, block, ports_int, ports_int, pltpu.VMEM((1, HALF), F32),
            line_int, line_int, line, hist_shape, pay_scratch, side, side, pltpu.SemaphoreType.DMA((15,)),
        ],
        name="first",
    )
    got = exchanged(pay)
    e, h, d, g, pre, state = call(
        k_start,
        [E_SHAPE, H_SHAPE, WIDE, WIDE, (8, LANES), (ROWS, LANES)],
        e_field, h_field, e_decay, e_gain, port_cell, line_near, line_delay, line_imped, hist_near, hist_far,
        shifted(to_right, "fxy", 1), shifted(to_left, "fxy", -1),
        shifted(below, "fz", 1), shifted_up(corner_right, 1), shifted_up(corner_left, -1),
        far=range(12),
        far_out=(2, 3),
        scratch=[side, side, wide, wide, ports_int, line_int, line_int, line, hist_shape, hist_shape, pltpu.SemaphoreType.DMA((14,))],
        name="start",
    )
    pay, state = call(
        k_tables,
        [PAY_SHAPE, (ROWS, LANES)],
        got, pre, inverse, state,
        alias={3: 1},
        far=(2,),
        far_out=(0,),
        scratch=[pltpu.VMEM((1, LANES, NB * LANES), F32), pay_scratch, pltpu.SemaphoreType.DMA((2,))],
        name="tables",
    )
    for n in range(STEPS):
        last = n == STEPS - 1
        got = exchanged(pay)
        (e,) = call(k_exy, [E_SHAPE], h, d, g, e, alias={3: 0}, name="exy")
        e, state, *sends = call(
            functools.partial(k_currents, n, last),
            [E_SHAPE, (ROWS, LANES)] + ([] if last else [UP_SHAPE]) + [DOWN_SHAPE],
            got, e, state,
            alias={1: 0, 2: 1},
            name="currents",
        )
        down = shifted(sends[-1], "fz", -1)
        if last:
            break
        up = shifted(sends[0], "fz", 1)
        (h,) = call(k_inner_h, [H_SHAPE], e, h, alias={1: 0}, name="inner_h")
        e, h, state, pay, *node_volt = call(
            functools.partial(k_volts, n + 1, n + 1 == STEPS - 1),
            [E_SHAPE, H_SHAPE, (ROWS, LANES), PAY_SHAPE] + ([(1, LANES)] if n + 1 == STEPS - 1 else []),
            up, down, d, g, inverse, port_cell, e, h, state,
            alias={6: 0, 7: 1, 8: 2},
            far_out=(3, 4) if n + 1 == STEPS - 1 else (3,),
            scratch=([line, pltpu.SemaphoreType.DMA] if n + 1 == STEPS - 1 else []) + [pay_scratch, pltpu.SemaphoreType.DMA],
            name="volts",
        )
    h, e_out, h_out = call(
        k_inner_last,
        [H_SHAPE, FIELD, FIELD],
        e, h,
        alias={1: 0},
        far_out=(1, 2),
        scratch=[pltpu.SemaphoreType.DMA((2,))],
        name="inner_last",
    )
    h_out, line_wave = call(
        k_last,
        [FIELD, (1, 2, LANES)],
        down, state, e, h, h_out,
        alias={4: 0},
        far=(4,),
        far_out=(0, 1),
        scratch=[pltpu.VMEM((3, NX, NY), F32), pltpu.VMEM((1, 2, LANES), F32), pltpu.SemaphoreType.DMA((2,))],
        name="last",
    )
    return e_out, h_out, node_volt[0], line_wave


def solution(mesh):
    placed = (
        P(None, "fz", "fxy", None),
        P(None, "fz", "fxy", None),
        P("fz", "fxy", None),
        P("fz", "fxy", None),
        P("fz", "fxy"),
        P("fz", "fxy"),
        P("fz", "fxy"),
        P("fz", "fxy", None),
        P("fz", None),
        P("fz", None),
        P("fz", None),
        P("fz", None),
        P("fz", None, None),
        P("fz", None, None),
    )
    return jax.shard_map(
        local,
        mesh=mesh,
        in_specs=placed,
        out_specs=(
            P(None, "fz", "fxy", None),
            P(None, "fz", "fxy", None),
            P("fz", "fxy"),
            P("fz", None, None),
        ),
        check_vma=False,
    )
```

```python
import functools

import jax
import jax.numpy as jnp
from jax import lax
from jax.experimental import pallas as pl
from jax.experimental.pallas import tpu as pltpu
from jax.sharding import PartitionSpec as P

STEPS = 4
F32 = jnp.float32
BF16 = jnp.bfloat16
NZ = 8
NX = 16
NY = 512
GX = 24
DEEP = 4
NF = 32
NB = 16
HALF = 64
LANES = 128
DEPTH = 6
VMEM = pl.BlockSpec(memory_space=pltpu.VMEM)
ANY = pl.BlockSpec(memory_space=pltpu.HBM)
NT = (((1,), (1,)), ((), ()))
NODE, WHERE, COND, GAIN, EZ, STATIC, OWN, FROM_ABOVE, FROM_BELOW, WAVE, ROWS = 0, 16, 24, 32, 40, 48, 56, 72, 88, 104, 112
E_SHAPE = (3, NZ + 2, GX, NY)
H_SHAPE = (3, NZ + 1, GX, NY)
PAY_SHAPE = (NB, 2, LANES)
LAYERS = 8 * NZ
SIDE_SHAPE = (LAYERS * DEEP, NY)
WIDE = (NZ, GX, NY)
UP_SHAPE, DOWN_SHAPE, TOP_SHAPE = (3 * GX + 8, NY), (2 * GX + 8, NY), (2 * GX, NY)
LINES_SHAPE = (8, 2 * LANES)
FIELD = (3, NZ, NX, NY)


def call(kernel, outs, *args, alias=None, name=None, far=(), far_out=(), scratch=(), room=40 << 20):
    args = [pltpu.with_memory_space_constraint(x, pltpu.HBM) if k in far else x for k, x in enumerate(args)]
    return pl.pallas_call(
        kernel,
        out_shape=[pltpu.HBM(s, F32) if k in far_out else jax.ShapeDtypeStruct(s, F32) for k, s in enumerate(outs)],
        in_specs=[ANY if k in far else VMEM for k in range(len(args))],
        out_specs=[ANY if k in far_out else VMEM for k in range(len(outs))],
        scratch_shapes=list(scratch),
        input_output_aliases=alias or {},
        name=name,
        compiler_params=pltpu.CompilerParams(vmem_limit_bytes=room),
    )(*args)


def shifted(value, axis, by):
    devices = lax.axis_size(axis)
    pairs = [(i, i + by) for i in range(devices) if 0 <= i + by < devices]
    return lax.ppermute(value, axis, pairs)


def exchanged(value):
    return lax.all_to_all(value, "fxy", 0, 0, tiled=True)


def iota(shape, dim):
    return lax.broadcasted_iota(jnp.int32, shape, dim)


def column():
    return lax.axis_index("fxy")


def row():
    return lax.axis_index("fz")


def split3(value):
    high = value.astype(BF16)
    rest = value - high.astype(F32)
    middle = rest.astype(BF16)
    low = (rest - middle.astype(F32)).astype(BF16)
    return high, middle, low


def dot3(value, onehot, dims=(((1,), (0,)), ((), ()))):
    rows = value.shape[0]
    parts = jnp.concatenate(split3(value), 0)
    product = lax.dot_general(parts, onehot, dims, preferred_element_type=F32)
    return product[:rows] + (product[rows : 2 * rows] + product[2 * rows :])


def ones_where(condition):
    return jnp.where(condition, 1.0, 0.0).astype(BF16)


def next_y(f):
    rolled = pltpu.roll(f, NY - 1, 1)
    return jnp.where(iota(f.shape, 1) == NY - 1, 0.0, rolled)


def last_y(f):
    rolled = pltpu.roll(f, 1, 1)
    return jnp.where(iota(f.shape, 1) == 0, 0.0, rolled)


def next_x(f):
    return jnp.concatenate([f[1:], f[:1]], 0)


def last_x(f):
    return jnp.concatenate([f[GX - 1 :], f[: GX - 1]], 0)


def copies(pairs, sems):
    started = [pltpu.make_async_copy(a, b, sems.at[k]) for k, (a, b) in enumerate(pairs)]
    for copy in started:
        copy.start()
    return started


def wait(started):
    for copy in started:
        copy.wait()


def lower(got_ref, f):
    lane = iota((8, LANES), 1)
    return jnp.where(lane < HALF, got_ref[0:8, f, :], pltpu.roll(got_ref[8:16, f, :], HALF, 1))


def upper(got_ref, f):
    lane = iota((8, LANES), 1)
    return jnp.where(lane < HALF, pltpu.roll(got_ref[0:8, f, :], HALF, 1), got_ref[8:16, f, :])


def own_ports(cell):
    cell = jnp.concatenate([cell, cell], 1)
    mine = iota((1, LANES), 1) < HALF
    at_row = ones_where((iota((NZ * NX, LANES), 0) == cell // NY) & mine)
    at_y = ones_where(iota((NY, LANES), 0) == cell % NY)
    return at_row, at_y


def at_ports(field, ports):
    at_row, at_y = ports
    return jnp.sum(dot3(field, at_y) * at_row.astype(F32), 0, keepdims=True)


def hist_at(hist, position):
    out = jnp.zeros((1, LANES), F32)
    for k in range(DEPTH + STEPS):
        out = jnp.where(position == k, hist[k : k + 1], out)
    return out


def k_first(
    e_in, h_in, d_in, g_in, cell_ref, node_ref, cond_ref, far_ref, delay_ref, imped_ref, near_hist_ref,
    pay_out, lines_ref, right_out, left_out,
    e_ref, h_ref, d_ref, g_ref, cell, node, cond, far, delay, imped, hist, pay_ref, right_ref, left_ref, sems,
):
    pairs = [
        (cell_ref, cell), (node_ref, node), (cond_ref, cond), (e_in.at[2], e_ref.at[2]),
        (e_in.at[0:2], e_ref.at[0:2]), (h_in, h_ref), (d_in, d_ref), (g_in, g_ref),
        (far_ref, far), (delay_ref, delay), (imped_ref, imped), (near_hist_ref, hist),
    ]
    started = copies(pairs, sems)
    lines_ref[...] = jnp.zeros(LINES_SHAPE, F32)
    wait(started[:4])
    here = at_ports(e_ref[2].reshape(NZ * NX, NY), own_ports(cell[...]))
    first = jnp.concatenate([node[...], cell[...]], 1).astype(F32)
    second = jnp.concatenate([cond[...], here[:, :HALF]], 1)
    sending = [payload(pay_out, pay_ref, sems.at[12], first, second)]
    wait(started[4:8])
    layers = [(ref, (c, z)) for ref in (e_ref, h_ref) for c in range(3) for z in range(NZ)]
    layers += [(ref, (z,)) for ref in (d_ref, g_ref) for z in range(NZ)]
    for k in range(0, LAYERS, 2):
        tiles = [ref[(*at, slice(NX - 8, NX))] for ref, at in layers[k : k + 2]]
        right_ref[k * DEEP : (k + 2) * DEEP] = jnp.concatenate([t[DEEP:] for t in tiles], 0)
        tiles = [ref[(*at, slice(0, 8))] for ref, at in layers[k : k + 2]]
        left_ref[k * DEEP : (k + 2) * DEEP] = jnp.concatenate([t[:DEEP] for t in tiles], 0)
    for k, (a, b) in enumerate(((right_ref, right_out), (left_ref, left_out))):
        sending.append(pltpu.make_async_copy(a, b, sems.at[13 + k]))
        sending[-1].start()
    wait(started[8:])
    lines_ref[0:1, 0:LANES] = far[...].astype(F32)
    lines_ref[1:2, 0:LANES] = delay[...].astype(F32)
    lines_ref[2:3, 0:LANES] = imped[...]
    for k in range(DEPTH):
        lines_ref[k : k + 1, LANES:] = hist[k]
    wait(sending)


def update_e(e_ref, h_ref, d_ref, g_ref, components, width):
    for z in range(NZ):
        hx, hy, hz = h_ref[0, z + 1], h_ref[1, z + 1], h_ref[2, z + 1]
        d, g = d_ref[z], g_ref[z]
        for c in components:
            if c == 0:
                own = hz[:width]
                curl = (own - last_y(own)) - (hy[:width] - h_ref[1, z, :width])
            elif c == 1:
                curl = (hx[:width] - h_ref[0, z, :width]) - (hz - last_x(hz))[:width]
            else:
                own = hx[:width]
                curl = (hy - last_x(hy))[:width] - (own - last_y(own))
            e_ref[c, z + 1, :width] = d * e_ref[c, z + 1, :width] + g * curl


def own_rows(ref):
    return ref.at[:, 1 : NZ + 1, 0:NX]


def k_start(
    e_in, h_in, d_in, g_in, right_ref, left_ref, cell_in, lines_ref, e_ref, h_ref, d_out, g_out, pre_ref, top_ref,
    d_ref, g_ref, cell_ref, sems,
):
    pairs = [
        (d_in, d_ref.at[:, 0:NX]), (g_in, g_ref.at[:, 0:NX]), (e_in, own_rows(e_ref)), (h_in, own_rows(h_ref)), (cell_in, cell_ref),
    ]
    started = copies(pairs, sems)
    for c in range(3):
        h_ref[c, 0] = jnp.zeros((GX, NY), F32)
        e_ref[c, 0] = jnp.zeros((GX, NY), F32)
        e_ref[c, NZ + 1] = jnp.zeros((GX, NY), F32)

    def tile(k):
        rows = slice(k * DEEP, (k + 1) * DEEP)
        return jnp.concatenate([left_ref[rows], right_ref[rows]], 0)

    for z in range(NZ):
        d_ref[z, NX:] = tile(6 * NZ + z)
        g_ref[z, NX:] = tile(7 * NZ + z)
    wait(started[:2])
    more = [pltpu.make_async_copy(d_ref, d_out, sems.at[5]), pltpu.make_async_copy(g_ref, g_out, sems.at[6])]
    for copy in more:
        copy.start()
    for c in range(3):
        for z in range(NZ):
            e_ref[c, z + 1, NX:] = tile(c * NZ + z)
            h_ref[c, z + 1, NX:] = tile(3 * NZ + c * NZ + z)
    wait(started[2:])
    update_e(e_ref, h_ref, d_ref, g_ref, (2,), GX)
    for c in range(2):
        top_ref[c * GX : (c + 1) * GX] = h_ref[c, NZ]
    ports = own_ports(cell_ref[...])
    pre = at_ports(e_ref[2, 1 : NZ + 1, :NX].reshape(NZ * NX, NY), ports)
    gain = at_ports(g_ref[:, :NX].reshape(NZ * NX, NY), ports)
    pre_ref[...] = jnp.broadcast_to(pre + pltpu.roll(gain, HALF, 1), (8, LANES))
    wait(more)


def low_onehots(node):
    return jnp.concatenate([ones_where(iota((LANES, LANES), 0) == node[t : t + 1] % LANES) for t in range(10)], 1)


def own_volts(w, lines, node, inverse_ref):
    high = node // LANES
    values = jnp.concatenate([w, lines], 0)
    spread = [jnp.where(iota((NB, LANES), 0) == high[t : t + 1], values[t : t + 1], 0.0) for t in range(10)]
    sources = dot3(jnp.concatenate(spread, 1), low_onehots(node), NT)
    total = jnp.zeros((LANES, LANES), F32)
    for t in range(NB):
        total = total + inverse_ref[0, :, t * LANES : (t + 1) * LANES] * sources[t : t + 1]
    return jnp.sum(total.T, 0, keepdims=True)


def node_values(volts, node):
    high = node // LANES
    picked = dot3(volts, low_onehots(node))
    rows = []
    for t in range(10):
        mine = jnp.where(iota((NB, LANES), 0) == high[t : t + 1], picked[:, t * LANES : (t + 1) * LANES], 0.0)
        rows.append(jnp.sum(mine, 0, keepdims=True))
    return jnp.concatenate(rows, 0)


def line_inputs(state_ref, n):
    own = n - state_ref[STATIC + 4 : STATIC + 5].astype(jnp.int32) + DEPTH
    below = n - state_ref[STATIC + 5 : STATIC + 6].astype(jnp.int32) + DEPTH
    return (
        hist_at(state_ref[FROM_ABOVE : FROM_ABOVE + 16], own),
        hist_at(state_ref[FROM_BELOW : FROM_BELOW + 16], below),
        hist_at(state_ref[OWN : OWN + 16], own),
    )


def next_volts(state_ref, inverse_ref, n):
    into_near, into_below, _ = line_inputs(state_ref, n)
    lines = -jnp.concatenate([into_near, into_below], 0)
    w = state_ref[COND : COND + 8] * state_ref[EZ : EZ + 8]
    return own_volts(w, lines, state_ref[NODE : NODE + 16].astype(jnp.int32), inverse_ref)


def payload(pay_out, pay_ref, sem, volts, pre):
    pay_ref[...] = jnp.broadcast_to(jnp.concatenate([volts, pre], 0)[None], PAY_SHAPE)
    copy = pltpu.make_async_copy(pay_ref, pay_out, sem)
    copy.start()
    return copy


def k_tables(
    got_ref, lines_ref, pre_ref, near_in, delay_in, imped_in, near_hist_in, far_hist_in, inverse_in,
    pay_out, state_ref,
    near_ref, delay_ref, imped_ref, near_hist_ref, far_hist_ref, inverse_ref, pay_ref, sems,
):
    pairs = [
        (near_in, near_ref), (delay_in, delay_ref), (imped_in, imped_ref),
        (near_hist_in, near_hist_ref), (far_hist_in, far_hist_ref), (inverse_in, inverse_ref),
    ]
    started = copies(pairs, sems)
    state_ref[...] = jnp.zeros((ROWS, LANES), F32)
    state_ref[NODE : NODE + 8] = lower(got_ref, 0)
    device = iota((8, LANES), 0) + 8 * (iota((8, LANES), 1) // HALF)
    state_ref[WHERE : WHERE + 8] = upper(got_ref, 0) + (device * (NZ * NX * NY)).astype(F32)
    state_ref[COND : COND + 8] = lower(got_ref, 1)
    state_ref[EZ : EZ + 8] = upper(got_ref, 1)
    far_below = lines_ref[0:1, 0:LANES]
    imped_below = jnp.where(row() == 0, 1.0, lines_ref[2:3, 0:LANES])
    wait(started[:5])
    near = near_ref[...].astype(F32)
    static = [near, far_below, imped_ref[...], imped_below, delay_ref[...].astype(F32), lines_ref[1:2, 0:LANES]]
    state_ref[NODE + 8 : NODE + 10] = jnp.concatenate(static[:2], 0)
    state_ref[STATIC : STATIC + 6] = jnp.concatenate(static, 0)
    for k in range(DEPTH):
        back = DEPTH - 1 - k
        state_ref[OWN + k : OWN + k + 1] = near_hist_ref[back]
        state_ref[FROM_ABOVE + k : FROM_ABOVE + k + 1] = far_hist_ref[back]
        state_ref[FROM_BELOW + k : FROM_BELOW + k + 1] = lines_ref[back : back + 1, LANES:]
    wait(started[5:])
    payload(pay_out, pay_ref, sems.at[6], next_volts(state_ref, inverse_ref, 0), pre_ref[0:1]).wait()


def block_row(k):
    block = column() + k
    return jnp.where(block < 0, block + 8, block % 8), block // 8, (block >= 0) & (block < NB)


def spread_currents(e_ref, where, drop):
    row_parts, at_y = [], []
    for k in (-1, 0, 1):
        packed, half, exists = block_row(k)
        pick = iota((8, LANES), 0) == packed
        cell = jnp.sum(jnp.where(pick, where, 0.0), 0, keepdims=True).astype(jnp.int32) % (NZ * NX * NY)
        values = jnp.sum(jnp.where(pick, drop, 0.0), 0, keepdims=True)
        x = (cell // NY) % NX + k * NX
        position = jnp.where((x >= 0) & (x < NX + DEEP), x, jnp.where((x < 0) & (x >= -DEEP), x + GX, -1))
        inside = (iota((1, LANES), 1) // HALF == half) & exists & (position >= 0)
        target = jnp.where(inside, (cell // (NX * NY)) * GX + position, -1)
        at_row = ones_where(iota((NZ * GX, LANES), 0) == target)
        row_parts.append(jnp.concatenate([at_row * part for part in split3(values)], 0))
        at_y.append(ones_where(iota((NY, LANES), 0) == cell % NY))
    spread = lax.dot_general(jnp.concatenate(row_parts, 1), jnp.concatenate(at_y, 1), NT, preferred_element_type=F32)
    rows = NZ * GX
    spread = spread[:rows] + (spread[rows : 2 * rows] + spread[2 * rows :])
    for z in range(NZ):
        e_ref[2, z + 1] = e_ref[2, z + 1] - spread[z * GX : (z + 1) * GX]


def k_currents(n, last, got_ref, e_in, state_in, e_ref, state_ref, *sends):
    pre = lower(got_ref, 1)
    if n == 0:
        state_ref[GAIN : GAIN + 8] = upper(got_ref, 1)
    at_nodes = node_values(got_ref[:, 0, :], state_ref[NODE : NODE + 16].astype(jnp.int32))
    where = state_ref[WHERE : WHERE + 8]
    current = state_ref[COND : COND + 8] * (state_ref[EZ : EZ + 8] - at_nodes[0:8])
    shared = current
    for k in range(1, LANES):
        same = pltpu.roll(where, k, 1) == where
        shared = shared + jnp.where(same, pltpu.roll(current, k, 1), 0.0)
    gain = state_ref[GAIN : GAIN + 8]
    state_ref[EZ : EZ + 8] = pre - gain * shared

    into_near, into_below, into_own = line_inputs(state_ref, n)
    out_near = -2.0 * at_nodes[8:9] / state_ref[STATIC + 2 : STATIC + 3] - into_near
    out_below = -2.0 * at_nodes[9:10] / state_ref[STATIC + 3 : STATIC + 4] - into_below
    top = jnp.where(row() == NF - 1, -into_own, 0.0)
    state_ref[WAVE : WAVE + 2] = jnp.concatenate([out_near, top], 0)

    spread_currents(e_ref, where, gain * current)

    down_ref = sends[-1]
    for c in range(2):
        down_ref[c * GX : (c + 1) * GX] = e_ref[c, 1]
    down_ref[2 * GX :] = jnp.zeros((8, NY), F32)
    down_ref[2 * GX : 2 * GX + 1, 0:LANES] = out_below
    if not last:
        up_ref = sends[0]
        for c in range(3):
            up_ref[c * GX : (c + 1) * GX] = e_ref[c, NZ]
        up_ref[3 * GX :] = jnp.zeros((8, NY), F32)
        up_ref[3 * GX : 3 * GX + 1, 0:LANES] = out_near


def new_h(e_ref, h_ref, layer, ex_above, ey_above):
    scale = jnp.where((iota((GX, 1), 0) >= GX - DEEP) & (column() == 0), 0.0, 0.5)
    ex, ey, ez = e_ref[0, layer], e_ref[1, layer], e_ref[2, layer]
    if layer == 0:
        scale = jnp.where(row() == 0, 0.0, scale)
    hx = h_ref[0, layer] - scale * ((next_y(ez) - ez) - (ey_above - ey))
    hy = h_ref[1, layer] - scale * ((ex_above - ex) - (next_x(ez) - ez))
    hz = h_ref[2, layer] - scale * ((next_x(ey) - ey) - (next_y(ex) - ex))
    return hx, hy, hz


def update_h(e_ref, h_ref, layer):
    for c, value in enumerate(new_h(e_ref, h_ref, layer, e_ref[0, layer + 1], e_ref[1, layer + 1])):
        h_ref[c, layer] = value


def k_inner_h(e_ref, h_in, h_ref):
    for layer in range(1, NZ):
        update_h(e_ref, h_ref, layer)


def k_inner_last(e_ref, h_in, h_ref, e_out, h_out, sems):
    first = copies([(own_rows(e_ref), e_out)], sems)
    for layer in range(1, NZ):
        update_h(e_ref, h_ref, layer)
    second = pltpu.make_async_copy(h_ref.at[:, 1:NZ, 0:NX], h_out.at[:, 0 : NZ - 1], sems.at[1])
    second.start()
    wait(first)
    second.wait()


def k_volts(
    n, last, up_ref, down_ref, d_ref, g_ref, inverse_ref, cell_ref, e_in, h_in, state_in,
    e_ref, h_ref, state_ref, pay_out, *rest,
):
    pay_ref, sem = rest[-2:]
    at = n - 1 + DEPTH
    state_ref[OWN + at : OWN + at + 1] = state_ref[WAVE : WAVE + 1]
    state_ref[FROM_ABOVE + at : FROM_ABOVE + at + 1] = down_ref[2 * GX : 2 * GX + 1, 0:LANES] + state_ref[WAVE + 1 : WAVE + 2]
    state_ref[FROM_BELOW + at : FROM_BELOW + at + 1] = up_ref[3 * GX : 3 * GX + 1, 0:LANES]
    volts = next_volts(state_ref, inverse_ref, n)
    if last:
        rest[1][...] = volts
        sending = pltpu.make_async_copy(rest[1], rest[0], rest[2])
        sending.start()
    for c in range(3):
        e_ref[c, 0] = up_ref[c * GX : (c + 1) * GX]
    for c in range(2):
        e_ref[c, NZ + 1] = down_ref[c * GX : (c + 1) * GX]
    update_h(e_ref, h_ref, 0)
    update_h(e_ref, h_ref, NZ)
    update_e(e_ref, h_ref, d_ref, g_ref, (2,), GX)
    pre = at_ports(e_ref[2, 1 : NZ + 1, :NX].reshape(NZ * NX, NY), own_ports(cell_ref[...]))
    payload(pay_out, pay_ref, sem, volts, pre).wait()
    if last:
        sending.wait()


def k_exy_first(top_ref, d_ref, g_ref, e_in, h_in, e_ref, h_ref):
    for c in range(2):
        h_ref[c, 0] = top_ref[c * GX : (c + 1) * GX]
    update_e(e_ref, h_ref, d_ref, g_ref, (0, 1), GX)


def k_exy(h_ref, d_ref, g_ref, e_in, e_ref):
    update_e(e_ref, h_ref, d_ref, g_ref, (0, 1), GX)


def k_last(down_ref, state_ref, e_ref, h_ref, h_in, h_out, wave_out, layer_ref, wave_ref, sems):
    above = down_ref[2 * GX : 2 * GX + 1, 0:LANES] + state_ref[WAVE + 1 : WAVE + 2]
    wave_ref[...] = jnp.concatenate([state_ref[WAVE : WAVE + 1], above], 0)[None]
    sending = copies([(wave_ref, wave_out)], sems)
    for c, value in enumerate(new_h(e_ref, h_ref, NZ, down_ref[0:GX], down_ref[GX : 2 * GX])):
        layer_ref[c] = value[:NX]
    sending.append(pltpu.make_async_copy(layer_ref, h_out.at[:, NZ - 1], sems.at[1]))
    sending[1].start()
    wait(sending)


def local(
    e_field,
    h_field,
    e_decay,
    e_gain,
    port_cell,
    port_node,
    port_conductance,
    inverse,
    line_near,
    line_far,
    line_delay,
    line_imped,
    hist_near,
    hist_far,
):
    hist_near = jnp.transpose(hist_near, (1, 0, 2))
    hist_far = jnp.transpose(hist_far, (1, 0, 2))
    hist_shape = pltpu.VMEM((DEPTH, 1, LANES), F32)
    line = pltpu.VMEM((1, LANES), F32)
    line_int = pltpu.VMEM((1, LANES), jnp.int32)
    ports_int = pltpu.VMEM((1, HALF), jnp.int32)
    block = pltpu.VMEM((NZ, NX, NY), F32)
    pay_scratch = pltpu.VMEM(PAY_SHAPE, F32)
    side = pltpu.VMEM(SIDE_SHAPE, F32)
    wide = pltpu.VMEM(WIDE, F32)

    pay, lines, to_right, to_left = call(
        k_first,
        [PAY_SHAPE, LINES_SHAPE, SIDE_SHAPE, SIDE_SHAPE],
        e_field, h_field, e_decay, e_gain, port_cell, port_node, port_conductance, line_far, line_delay, line_imped, hist_near,
        far=range(11),
        far_out=(0, 2, 3),
        scratch=[
            pltpu.VMEM(FIELD, F32), pltpu.VMEM(FIELD, F32), block, block, ports_int, ports_int, pltpu.VMEM((1, HALF), F32),
            line_int, line_int, line, hist_shape, pay_scratch, side, side, pltpu.SemaphoreType.DMA((15,)),
        ],
        name="first",
    )
    got = exchanged(pay)
    lines = shifted(lines, "fz", 1)
    e, h, d, g, pre, top = call(
        k_start,
        [E_SHAPE, H_SHAPE, WIDE, WIDE, (8, LANES), TOP_SHAPE],
        e_field, h_field, e_decay, e_gain, shifted(to_right, "fxy", 1), shifted(to_left, "fxy", -1), port_cell, lines,
        far=(0, 1, 2, 3, 6),
        far_out=(2, 3),
        scratch=[wide, wide, ports_int, pltpu.SemaphoreType.DMA((7,))],
        name="start",
    )
    pay, state = call(
        k_tables,
        [PAY_SHAPE, (ROWS, LANES)],
        got, lines, pre, line_near, line_delay, line_imped, hist_near, hist_far, inverse,
        far=range(3, 9),
        scratch=[
            line_int, line_int, line, hist_shape, hist_shape,
            pltpu.VMEM((1, LANES, NB * LANES), F32), pay_scratch, pltpu.SemaphoreType.DMA((7,)),
        ],
        far_out=(0,),
        name="tables",
    )
    for n in range(STEPS):
        last = n == STEPS - 1
        got = exchanged(pay)
        if n == 0:
            e, h = call(
                k_exy_first,
                [E_SHAPE, H_SHAPE],
                shifted(top, "fz", 1), d, g, e, h,
                alias={3: 0, 4: 1},
                name="exy_first",
            )
        else:
            (e,) = call(k_exy, [E_SHAPE], h, d, g, e, alias={3: 0}, name="exy")
        e, state, *sends = call(
            functools.partial(k_currents, n, last),
            [E_SHAPE, (ROWS, LANES)] + ([] if last else [UP_SHAPE]) + [DOWN_SHAPE],
            got, e, state,
            alias={1: 0, 2: 1},
            name="currents",
        )
        down = shifted(sends[-1], "fz", -1)
        if last:
            break
        up = shifted(sends[0], "fz", 1)
        (h,) = call(k_inner_h, [H_SHAPE], e, h, alias={1: 0}, name="inner_h")
        e, h, state, pay, *node_volt = call(
            functools.partial(k_volts, n + 1, n + 1 == STEPS - 1),
            [E_SHAPE, H_SHAPE, (ROWS, LANES), PAY_SHAPE] + ([(1, LANES)] if n + 1 == STEPS - 1 else []),
            up, down, d, g, inverse, port_cell, e, h, state,
            alias={6: 0, 7: 1, 8: 2},
            far_out=(3, 4) if n + 1 == STEPS - 1 else (3,),
            scratch=([line, pltpu.SemaphoreType.DMA] if n + 1 == STEPS - 1 else []) + [pay_scratch, pltpu.SemaphoreType.DMA],
            name="volts",
        )
    h, e_out, h_out = call(
        k_inner_last,
        [H_SHAPE, FIELD, FIELD],
        e, h,
        alias={1: 0},
        far_out=(1, 2),
        scratch=[pltpu.SemaphoreType.DMA((2,))],
        name="inner_last",
    )
    h_out, line_wave = call(
        k_last,
        [FIELD, (1, 2, LANES)],
        down, state, e, h, h_out,
        alias={4: 0},
        far=(4,),
        far_out=(0, 1),
        scratch=[pltpu.VMEM((3, NX, NY), F32), pltpu.VMEM((1, 2, LANES), F32), pltpu.SemaphoreType.DMA((2,))],
        name="last",
    )
    return e_out, h_out, node_volt[0], line_wave


def solution(mesh):
    placed = (
        P(None, "fz", "fxy", None),
        P(None, "fz", "fxy", None),
        P("fz", "fxy", None),
        P("fz", "fxy", None),
        P("fz", "fxy"),
        P("fz", "fxy"),
        P("fz", "fxy"),
        P("fz", "fxy", None),
        P("fz", None),
        P("fz", None),
        P("fz", None),
        P("fz", None),
        P("fz", None, None),
        P("fz", None, None),
    )
    return jax.shard_map(
        local,
        mesh=mesh,
        in_specs=placed,
        out_specs=(
            P(None, "fz", "fxy", None),
            P(None, "fz", "fxy", None),
            P("fz", "fxy"),
            P("fz", None, None),
        ),
        check_vma=False,
    )
```
